32 devices in a mesh: dp: 4 (over y, x), seq: 8 (over z, core).
Axes of the slice: x: 2, y: 2, z: 4, core: 2. Of those that a mesh axis runs over, the one named last changes fastest.
Arguments:
- inputs: float32 [3, 4, 1024, 2048], P(None, 'dp', 'seq'), may hold values from -6 to 6
- segment_ids: int32 [3, 4, 1024], P(None, 'dp', 'seq'), may hold values from 0 to 7, never falling along the last dimension, each value on 1 to 512 neighbouring positions
- cotangent: float32 [3, 4, 1024, 2048], P(None, 'dp', 'seq'), may hold values from -6 to 6
- mixer_gain: bfloat16 [2048], P(('dp', 'seq')), may hold values from 0.099609375 to 1.8984375
- input_proj: bfloat16 [2048, 2048], P(('dp', 'seq')), may hold values from -0.125 to 0.125
- forget_proj: bfloat16 [2048, 2048], P(('dp', 'seq')), may hold values from -0.125 to 0.125
- gate_proj: bfloat16 [2048, 2048], P(('dp', 'seq')), may hold values from -0.125 to 0.125
- floor_log: bfloat16 [2048], P(('dp', 'seq')), may hold values from -12 to -2
- output_gain: bfloat16 [2048], P(('dp', 'seq')), may hold values from 0.099609375 to 1.8984375
- output_proj: bfloat16 [2048, 2048], P(('dp', 'seq')), may hold values from -0.25 to 0.25
- dense_gain: bfloat16 [2048], P(('dp', 'seq')), may hold values from 0.099609375 to 1.8984375
- up_first: bfloat16 [2048, 5632], P(('dp', 'seq')), may hold values from -0.125 to 0.125
- up_second: bfloat16 [2048, 5632], P(('dp', 'seq')), may hold values from -0.125 to 0.125
- down_proj: bfloat16 [5632, 2048], P(('dp', 'seq')), may hold values from -0.15625 to 0.15625
Outputs:
- block_out: float32 [3, 4, 1024, 2048], P(None, 'dp', 'seq')
- input_grad: float32 [3, 4, 1024, 2048], P(None, 'dp', 'seq')
- mixer_gain_grad: float32 [2048], P(('dp', 'seq'))
- input_proj_grad: float32 [2048, 2048], P(('dp', 'seq'))
- forget_proj_grad: float32 [2048, 2048], P(('dp', 'seq'))
- gate_proj_grad: float32 [2048, 2048], P(('dp', 'seq'))
- floor_log_grad: float32 [2048], P(('dp', 'seq'))
- output_gain_grad: float32 [2048], P(('dp', 'seq'))
- output_proj_grad: float32 [2048, 2048], P(('dp', 'seq'))
- dense_gain_grad: float32 [2048], P(('dp', 'seq'))
- up_first_grad: float32 [2048, 5632], P(('dp', 'seq'))
- up_second_grad: float32 [2048, 5632], P(('dp', 'seq'))
- down_proj_grad: float32 [5632, 2048], P(('dp', 'seq'))
The draws below stay inside these ranges and needn't reach their ends.
Inputs may be any that keep to these rules, and one draw needn't show every extreme that they name: `segment_ids`: along each sequence the document numbers never fall; each document spans at most 512 tokens, and one spans exactly that many.
All inputs are finite; a program needn't handle non-finite values.
Results may differ from the reference program's by a relative error of at most 0.012.
Values may be sent and summed in bfloat16 or wider, within the bound.
A program may use at most 512 MiB of HBM per device.

```python
import math
import jax
import jax.numpy as jnp
import numpy as np
from jax import lax

D = 2048
FF = 5632
MB = 3
SEQS = 4
LEN = 1024
DOCS = 8


def draw_floor_log(key, part):
    key_pick, key_slow, key_fast = jax.random.split(key, 3)
    slow_share = 0.5
    chosen = jax.random.uniform(key_pick, (D,)) < slow_share
    slow_logs = jax.random.uniform(key_slow, (D,), jnp.float32, math.log(0.25 / LEN), math.log(2.0 / LEN))
    fast_logs = jax.random.uniform(key_fast, (D,), jnp.float32, math.log(2.0 / LEN), math.log(0.12))
    return jnp.where(chosen, slow_logs, fast_logs).astype(jnp.bfloat16)


def shard_levels(key, dims, pieces, low, top_value):
    def one(dim, shards_of):
        heights = jax.random.uniform(jax.random.fold_in(jax.random.fold_in(key, 6), dim), (shards_of,), jnp.float32, low / len(pieces), top_value / len(pieces))
        return jnp.repeat(jnp.exp(heights), dims[dim] // shards_of).reshape((-1,) + (1,) * (len(dims) - dim - 1))

    loudness = one(*pieces[0])
    for cut in pieces[1:]:
        loudness = loudness * one(*cut)
    return loudness


def split_up(amount, total, bound, slope):
    portions = [(1 << 20) // math.isqrt(rank ** slope) + 1 for rank in range(2, amount + 1)]
    rest, given = total - bound - (amount - 1), [1] * (amount - 1)
    while rest > 0:
        free = [i for i in range(amount - 1) if given[i] < bound]
        pool, left = sum([portions[i] for i in free]), rest
        for i in free:
            addition = min(bound - given[i], max(1, left * portions[i] // pool), rest)
            given[i] = given[i] + addition
            rest = rest - addition
    return np.array([bound] + given)


def uneven_parts(own_key, amount, total, limit, lean):
    if amount == 2:
        one = jax.random.randint(own_key, (), max(1, total - limit), min(limit, total - 1) + 1)
        return jnp.stack([one, total - one])
    tallies = jnp.asarray(split_up(amount, total, limit, lean), jnp.int32)
    twos = (amount - 1) // 2
    giver, receiver = tallies[1:1 + 2 * twos:2], tallies[2:2 + 2 * twos:2]
    room = jnp.minimum(giver - 1, limit - receiver)
    shifted = jax.random.randint(jax.random.fold_in(own_key, 1), (twos,), 0, 1 << 20) % (room + 1)
    tallies = tallies.at[1:1 + 2 * twos:2].set(giver - shifted).at[2:2 + 2 * twos:2].set(receiver + shifted)
    return tallies[jax.random.permutation(jax.random.fold_in(own_key, 2), amount)]


def normal_values(rng, extent, deviation, bound, cuts=(), kind=jnp.bfloat16):
    level = shard_levels(rng, extent, cuts, -0.22, 0.18) if cuts else 1.0
    drawn = jax.random.normal(rng, extent, jnp.float32) * deviation * level
    return jnp.minimum(jnp.maximum(drawn, -bound), bound).astype(kind)


def setup_inputs(seed: int = 0) -> dict:
    arg_keys = jax.random.split(jax.random.key(seed), 15)
    return {
        "inputs": normal_values(arg_keys[0], (MB, SEQS, LEN, D), 1.0, 6.0, ((1, 4), (2, 8)), jnp.float32),
        "segment_ids": jax.vmap(lambda own: jnp.searchsorted(jnp.cumsum(uneven_parts(own, DOCS, LEN, LEN // 2, 2)), jnp.arange(LEN), side="right"))(jax.random.split(arg_keys[1], MB * SEQS)).reshape((MB, SEQS, LEN)).astype(jnp.int32),
        "cotangent": normal_values(arg_keys[2], (MB, SEQS, LEN, D), 1.0, 6.0, ((1, 4), (2, 8)), jnp.float32),
        "mixer_gain": jnp.clip(1.0 + 0.18 * jax.random.normal(arg_keys[3], (D,), jnp.float32), 0.099609375, 1.8984375).astype(jnp.bfloat16),
        "input_proj": normal_values(arg_keys[4], (D, D), D ** -0.5, 0.125, ((0, 32),)),
        "forget_proj": normal_values(arg_keys[5], (D, D), D ** -0.5, 0.125, ((0, 32),)),
        "gate_proj": normal_values(arg_keys[6], (D, D), D ** -0.5, 0.125, ((0, 32),)),
        "floor_log": draw_floor_log(jax.random.fold_in(arg_keys[14], 71), 0),
        "output_gain": jnp.clip(1.0 + 0.18 * jax.random.normal(arg_keys[8], (D,), jnp.float32), 0.099609375, 1.8984375).astype(jnp.bfloat16),
        "output_proj": normal_values(arg_keys[9], (D, D), (D // 4) ** -0.5, 0.25, ((0, 32),)),
        "dense_gain": jnp.clip(1.0 + 0.18 * jax.random.normal(arg_keys[10], (D,), jnp.float32), 0.099609375, 1.8984375).astype(jnp.bfloat16),
        "up_first": normal_values(arg_keys[11], (D, FF), D ** -0.5, 0.125, ((0, 32),)),
        "up_second": normal_values(arg_keys[12], (D, FF), D ** -0.5, 0.125, ((0, 32),)),
        "down_proj": normal_values(arg_keys[13], (FF, D), (FF // 4) ** -0.5, 0.15625, ((0, 32),)),
    }


norm_eps = 1e-06

@jax.custom_vjp
def low(v):
    return lax.optimization_barrier(v.astype(jnp.bfloat16)).astype(jnp.float32)

@jax.custom_vjp
def low_back(v):
    return v

def low_keep(v):
    return (low(v), None)

def low_pass(kept, grad):
    return (grad,)

def back_keep(v):
    return (v, None)

def back_low(kept, grad):
    return (low(grad),)
low.defvjp(low_keep, low_pass)
low_back.defvjp(back_keep, back_low)

def project(values, weights):
    return jnp.einsum('bld,de->ble', values, weights, precision=lax.Precision.HIGHEST)

def affine_pairs(earlier, later):
    decay_one, state_one = earlier
    decay_two, state_two = later
    return (decay_one * decay_two, decay_two * state_one + state_two)

def rms_scale(values):
    return lax.rsqrt(lax.optimization_barrier(jnp.mean(values * values, axis=-1, keepdims=True)) + norm_eps)

def forward_block(params, tokens, segments):
    mixer_gain, input_proj, forget_proj, gate_proj, floor_log, output_gain, output_proj, dense_gain, up_first, up_second, down_proj = params
    normed_one = low(tokens * rms_scale(tokens) * mixer_gain)
    pre_input = low_back(project(normed_one, input_proj))
    pre_forget = low_back(project(normed_one, forget_proj))
    pre_gate = low_back(project(normed_one, gate_proj))
    leak = jnp.exp(floor_log) * jax.nn.sigmoid(-pre_forget)
    linked = jnp.concatenate([jnp.zeros((segments.shape[0], 1), jnp.float32), (segments[:, 1:] == segments[:, :-1]).astype(jnp.float32)], axis=1)
    decay = (1.0 - leak) * linked[:, :, None]
    scanned = lax.associative_scan(affine_pairs, (decay, leak * jax.nn.silu(pre_input)), axis=1)
    states = scanned[1]
    normed_state = states * rms_scale(states)
    mixed = low(normed_state * output_gain * jax.nn.silu(pre_gate))
    middle = tokens + low_back(project(mixed, output_proj))
    normed_two = low(middle * rms_scale(middle) * dense_gain)
    up_one = low_back(project(normed_two, up_first))
    up_two = low_back(project(normed_two, up_second))
    activated = low(jax.nn.silu(up_one) * up_two)
    return middle + low_back(project(activated, down_proj))

def reference(inputs, segment_ids, cotangent, mixer_gain, input_proj, forget_proj, gate_proj, floor_log, output_gain, output_proj, dense_gain, up_first, up_second, down_proj):
    params = tuple((weight.astype(jnp.float32) for weight in (mixer_gain, input_proj, forget_proj, gate_proj, floor_log, output_gain, output_proj, dense_gain, up_first, up_second, down_proj)))

    def micro_step(totals, batch):
        tokens, segments, grad_out = batch
        result, pullback = jax.vjp(lambda weights, values: forward_block(weights, values, segments), params, tokens)
        grad_params, grad_tokens = pullback(grad_out)
        return (jax.tree.map(jnp.add, totals, grad_params), (result, grad_tokens))
    start_totals = jax.tree.map(jnp.zeros_like, params)
    totals, outputs = lax.scan(micro_step, start_totals, (inputs, segment_ids, cotangent))
    block_out, input_grad = outputs
    return (block_out, input_grad, totals[0], totals[1], totals[2], totals[3], totals[4], totals[5], totals[6], totals[7], totals[8], totals[9], totals[10])
```

```python
import jax
import jax.numpy as jnp
from jax import lax
from jax.experimental import pallas as pl
from jax.experimental.pallas import tpu as pltpu
from jax.sharding import PartitionSpec as P

norm_eps = 1e-06
ALL = ("dp", "seq")
LANES = 128
SUB = 8


def silu_slope(values):
    logistic = jax.nn.sigmoid(values)
    return logistic * (1.0 + values * (1.0 - logistic))


def norm_back(upstream, scaled, factor):
    return factor * (upstream - scaled * jnp.mean(upstream * scaled, axis=-1, keepdims=True))


def dot(left, right):
    return jnp.dot(left, right, preferred_element_type=jnp.float32)


def contract_last(left, right):
    return lax.dot_general(
        left, right, (((1,), (1,)), ((), ())), preferred_element_type=jnp.float32
    )


def contract_rows(left, right):
    return lax.dot_general(
        left, right, (((0,), (0,)), ((), ())), preferred_element_type=jnp.float32
    )


def shift_down(values, amount, fill):
    rows = lax.broadcasted_iota(jnp.int32, values.shape, 0)
    return jnp.where(rows < amount, fill, pltpu.roll(values, amount, 0))


def shift_up(values, amount, fill):
    rows = lax.broadcasted_iota(jnp.int32, values.shape, 0)
    return jnp.where(
        rows >= SUB - amount, fill, pltpu.roll(values, SUB - amount, 0)
    )


def forward_scan_kernel(span_len, pre_input, pre_forget, floor, link, products, partial):
    tiles = span_len // SUB
    scale = jnp.exp(floor[...].astype(jnp.float32))
    width = pre_input.shape[1]
    groups = pre_input.shape[0] // span_len

    def group(g, _):
        def tile(i, carry):
            prod_in, state_in = carry
            rows = pl.ds(pl.multiple_of(g * span_len + i * SUB, SUB), SUB)
            value = pre_input[rows, :]
            leak = scale * jax.nn.sigmoid(-pre_forget[rows, :])
            decay = (1.0 - leak) * link[rows, :1]
            state = leak * value * jax.nn.sigmoid(value)
            for step in (1, 2, 4):
                state = decay * shift_down(state, step, 0.0) + state
                decay = decay * shift_down(decay, step, 1.0)
            state = decay * state_in + state
            decay = decay * prod_in
            products[rows, :] = decay
            partial[rows, :] = state
            return decay[SUB - 1 :, :], state[SUB - 1 :, :]

        lax.fori_loop(
            0, tiles, tile, (jnp.ones((1, width), jnp.float32), jnp.zeros((1, width), jnp.float32))
        )
        return 0

    lax.fori_loop(0, groups, group, 0)


def backward_scan_kernel(span_len, grad_states, pre_forget, floor, link, local, carry_mult, head):
    tiles = span_len // SUB
    scale = jnp.exp(floor[...].astype(jnp.float32))
    width = grad_states.shape[1]
    groups = grad_states.shape[0] // span_len

    def group(g, _):
        def tile(k, carry):
            prod_in, pass_in = carry
            i = tiles - 1 - k
            rows = pl.ds(pl.multiple_of(g * span_len + i * SUB, SUB), SUB)
            upstream = grad_states[rows, :]
            decay = (1.0 - scale * jax.nn.sigmoid(-pre_forget[rows, :])) * link[rows, :1]
            passed = decay * upstream
            for step in (1, 2, 4):
                passed = decay * shift_up(passed, step, 0.0) + passed
                decay = decay * shift_up(decay, step, 1.0)
            passed = decay * pass_in + passed
            decay = decay * prod_in
            local[rows, :] = upstream + shift_up(passed, 1, pass_in)
            carry_mult[rows, :] = shift_up(decay, 1, prod_in)
            return decay[:1, :], passed[:1, :]

        prod_out, pass_out = lax.fori_loop(
            0, tiles, tile, (jnp.ones((1, width), jnp.float32), jnp.zeros((1, width), jnp.float32))
        )
        head[pl.ds(g, 1), :] = pass_out
        return 0

    lax.fori_loop(0, groups, group, 0)


def scan_block(width):
    return 256 if width % 256 == 0 else width


def forward_scan(pre_all, floor, link, span_len, width):
    rows = pre_all.shape[0]
    block = scan_block(width)
    steps = width // block
    out = jax.ShapeDtypeStruct((rows, width), jnp.float32)
    return pl.pallas_call(
        lambda *refs: forward_scan_kernel(span_len, *refs),
        grid=(steps,),
        in_specs=[
            pl.BlockSpec((rows, block), lambda j: (0, j)),
            pl.BlockSpec((rows, block), lambda j: (0, j + steps)),
            pl.BlockSpec((1, block), lambda j: (0, j)),
            pl.BlockSpec((rows, LANES), lambda j: (0, 0)),
        ],
        out_specs=[pl.BlockSpec((rows, block), lambda j: (0, j))] * 2,
        out_shape=[out, out],
    )(pre_all, pre_all, floor, link)


def backward_scan(grad_states, pre_all, floor, link, span_len, width):
    rows = pre_all.shape[0]
    groups = rows // span_len
    block = scan_block(width)
    steps = width // block
    out = jax.ShapeDtypeStruct((rows, width), jnp.float32)
    return pl.pallas_call(
        lambda *refs: backward_scan_kernel(span_len, *refs),
        grid=(steps,),
        in_specs=[
            pl.BlockSpec((rows, block), lambda j: (0, j)),
            pl.BlockSpec((rows, block), lambda j: (0, j + steps)),
            pl.BlockSpec((1, block), lambda j: (0, j)),
            pl.BlockSpec((rows, LANES), lambda j: (0, 0)),
        ],
        out_specs=[pl.BlockSpec((rows, block), lambda j: (0, j))] * 2
        + [pl.BlockSpec((groups, block), lambda j: (0, j))],
        out_shape=[out, out, jax.ShapeDtypeStruct((groups, width), jnp.float32)],
    )(grad_states, pre_all, floor, link)


def entering_forward(mult, value):
    parts, place = lax.axis_size("seq"), lax.axis_index("seq")
    both = lax.all_gather(jnp.stack([mult, value]).astype(jnp.bfloat16), "seq").astype(jnp.float32)
    total = jnp.zeros_like(value)
    for k in range(parts - 1):
        total = jnp.where(k < place, both[k, 0] * total + both[k, 1], total)
    return total


def entering_backward(mult, value):
    parts, place = lax.axis_size("seq"), lax.axis_index("seq")
    both = lax.all_gather(jnp.stack([mult, value]).astype(jnp.bfloat16), "seq").astype(jnp.float32)
    total = jnp.zeros_like(value)
    for k in range(parts - 1, 0, -1):
        total = jnp.where(k > place, both[k, 0] * total + both[k, 1], total)
    return total


def gather_all(shard):
    return lax.all_gather(shard, ALL, axis=0, tiled=True)


def scatter_all(whole):
    return lax.psum_scatter(whole, ALL, scatter_dimension=0, tiled=True)


def shards(
    inputs,
    segment_ids,
    cotangent,
    mixer_gain,
    input_proj,
    forget_proj,
    gate_proj,
    floor_log,
    output_gain,
    output_proj,
    dense_gain,
    up_first,
    up_second,
    down_proj,
):
    width = inputs.shape[-1]
    hidden = up_first.shape[1]
    groups = inputs.shape[0] * inputs.shape[1]
    span_len = inputs.shape[2]
    rows_all = groups * span_len
    parts, place = lax.axis_size("seq"), lax.axis_index("seq")

    vectors = jnp.stack([mixer_gain, floor_log, output_gain, dense_gain], axis=1)
    vectors = jnp.pad(vectors, ((0, 0), (0, LANES - 4)))
    mix_full = gather_all(
        jnp.concatenate([input_proj, forget_proj, gate_proj, vectors], axis=1)
    )
    out_full = gather_all(output_proj)
    up_full = gather_all(jnp.concatenate([up_first, up_second], axis=1))
    down_full = gather_all(down_proj)
    gains = mix_full[:, 3 * width : 3 * width + 4].T
    mixer_gain_all = gains[0:1].astype(jnp.float32)
    floor_all = gains[1:2].astype(jnp.float32)
    out_gain_all = gains[2:3].astype(jnp.float32)
    dense_gain_all = gains[3:4].astype(jnp.float32)

    seg = segment_ids.reshape(groups, span_len)
    before = lax.ppermute(seg[:, -1:], "seq", [(i, i + 1) for i in range(parts - 1)])
    before = jnp.where(place == 0, -1, before)
    link = (seg == jnp.concatenate([before, seg[:, :-1]], axis=1)).astype(jnp.float32)
    link = jnp.broadcast_to(link.reshape(rows_all, 1), (rows_all, LANES))

    flat = inputs.reshape(rows_all, width)
    scale_one = lax.rsqrt(jnp.mean(flat * flat, axis=1, keepdims=True) + norm_eps)
    scaled_one = flat * scale_one
    normed_one = (scaled_one * mixer_gain_all).astype(jnp.bfloat16)
    pre_all = dot(normed_one, mix_full)
    pre_input = pre_all[:, :width]
    pre_forget = pre_all[:, width : 2 * width]
    pre_gate = pre_all[:, 2 * width : 3 * width]

    products, partial_state = forward_scan(pre_all, floor_all, link, span_len, width)
    products = products.reshape(groups, span_len, width)
    span_mult = products[:, -1]
    entering = entering_forward(
        span_mult, partial_state.reshape(groups, span_len, width)[:, -1]
    )
    states = products * entering[:, None, :] + partial_state.reshape(groups, span_len, width)
    states_flat = states.reshape(rows_all, width)
    state_scale = lax.rsqrt(jnp.mean(states_flat * states_flat, axis=1, keepdims=True) + norm_eps)
    normed_state = states_flat * state_scale
    gate_out = jax.nn.silu(pre_gate)
    mixed = (normed_state * out_gain_all * gate_out).astype(jnp.bfloat16)
    middle = flat + dot(mixed, out_full)
    scale_two = lax.rsqrt(jnp.mean(middle * middle, axis=1, keepdims=True) + norm_eps)
    scaled_two = middle * scale_two
    normed_two = (scaled_two * dense_gain_all).astype(jnp.bfloat16)
    up_both = dot(normed_two, up_full)
    up_one, up_two = up_both[:, :hidden], up_both[:, hidden:]
    activated = (jax.nn.silu(up_one) * up_two).astype(jnp.bfloat16)
    block_out = (middle + dot(activated, down_full)).reshape(inputs.shape)

    grad_flat = cotangent.reshape(rows_all, width)
    grad_dense = grad_flat.astype(jnp.bfloat16)
    grad_act = contract_last(grad_dense, down_full)
    grad_up = jnp.concatenate(
        [
            (grad_act * up_two * silu_slope(up_one)).astype(jnp.bfloat16),
            (grad_act * jax.nn.silu(up_one)).astype(jnp.bfloat16),
        ],
        axis=1,
    )
    grad_normed_two = contract_last(grad_up, up_full)
    gain_two = jnp.sum(grad_normed_two * scaled_two, axis=0)
    grad_middle = grad_flat + norm_back(grad_normed_two * dense_gain_all, scaled_two, scale_two)
    grad_mixer = grad_middle.astype(jnp.bfloat16)
    grad_mix_in = contract_last(grad_mixer, out_full)
    gain_out = jnp.sum(grad_mix_in * normed_state * gate_out, axis=0)
    grad_pre_gate = (
        grad_mix_in * normed_state * out_gain_all * silu_slope(pre_gate)
    ).astype(jnp.bfloat16)
    grad_states = norm_back(grad_mix_in * out_gain_all * gate_out, normed_state, state_scale)

    local_grad, carry_mult, head_grad = backward_scan(
        grad_states, pre_all, floor_all, link, span_len, width
    )
    arriving = entering_backward(span_mult, head_grad)
    adjoint = (
        local_grad.reshape(groups, span_len, width)
        + carry_mult.reshape(groups, span_len, width) * arriving[:, None, :]
    ).reshape(rows_all, width)
    previous = jnp.concatenate([entering[:, None, :], states[:, :-1]], axis=1)
    previous = previous.reshape(rows_all, width) * link[:, :1]
    leak = jnp.exp(floor_all) * jax.nn.sigmoid(-pre_forget)
    grad_forget = adjoint * (previous - jax.nn.silu(pre_input))
    grad_pre_input = (adjoint * leak * silu_slope(pre_input)).astype(jnp.bfloat16)
    grad_pre_forget = (grad_forget * leak * jax.nn.sigmoid(pre_forget)).astype(jnp.bfloat16)
    floor_sum = -jnp.sum(grad_forget * leak, axis=0)
    grad_pre = jnp.concatenate(
        [
            grad_pre_input,
            grad_pre_forget,
            grad_pre_gate,
            jnp.zeros((rows_all, LANES), jnp.bfloat16),
        ],
        axis=1,
    )
    block_all = contract_last(grad_pre, mix_full)
    gain_one = jnp.sum(block_all * scaled_one, axis=0)
    input_grad = (
        grad_middle + norm_back(block_all * mixer_gain_all, scaled_one, scale_one)
    ).reshape(inputs.shape)

    low = jnp.bfloat16
    vector_sums = jnp.stack([gain_one, floor_sum, gain_out, gain_two], axis=1)
    terms = scatter_all(
        jnp.concatenate(
            [
                contract_rows(normed_one, grad_pre[:, : 3 * width]).astype(low),
                contract_rows(mixed, grad_mixer).astype(low),
                contract_rows(normed_two, grad_up).astype(low),
                jnp.pad(vector_sums, ((0, 0), (0, LANES - 4))).astype(low),
            ],
            axis=1,
        )
    ).astype(jnp.float32)
    down_grad = scatter_all(contract_rows(activated, grad_dense).astype(low)).astype(jnp.float32)
    base = 4 * width + 2 * hidden
    return (
        block_out,
        input_grad,
        terms[:, base],
        terms[:, :width],
        terms[:, width : 2 * width],
        terms[:, 2 * width : 3 * width],
        terms[:, base + 1],
        terms[:, base + 2],
        terms[:, 3 * width : 4 * width],
        terms[:, base + 3],
        terms[:, 4 * width : 4 * width + hidden],
        terms[:, 4 * width + hidden : base],
        down_grad,
    )


def solution(mesh):
    whole = P(None, "dp", "seq", None)
    vector = P(ALL)
    matrix = P(ALL, None)
    return jax.shard_map(
        shards,
        mesh=mesh,
        in_specs=(
            whole,
            P(None, "dp", "seq"),
            whole,
            vector,
            matrix,
            matrix,
            matrix,
            vector,
            vector,
            matrix,
            vector,
            matrix,
            matrix,
            matrix,
        ),
        out_specs=(
            whole,
            whole,
            vector,
            matrix,
            matrix,
            matrix,
            vector,
            vector,
            matrix,
            vector,
            matrix,
            matrix,
            matrix,
        ),
        check_vma=False,
    )
```

```python
import functools

import jax
import jax.numpy as jnp
from jax import lax
from jax.experimental import pallas as pl
from jax.experimental.pallas import tpu as pltpu
from jax.sharding import PartitionSpec as P

norm_eps = 1e-06
ALL = ("dp", "seq")
LANES = 128
SUB = 8
MESH = pl.DeviceIdType.MESH
SLOTS = 2


def silu_slope(values):
    logistic = jax.nn.sigmoid(values)
    return logistic * (1.0 + values * (1.0 - logistic))


def norm_back(upstream, scaled, factor):
    return factor * (upstream - scaled * jnp.mean(upstream * scaled, axis=-1, keepdims=True))


def dot(left, right):
    return jnp.dot(left, right, preferred_element_type=jnp.float32)


def contract_last(left, right):
    return lax.dot_general(
        left, right, (((1,), (1,)), ((), ())), preferred_element_type=jnp.float32
    )


def contract_rows(left, right):
    return lax.dot_general(
        left, right, (((0,), (0,)), ((), ())), preferred_element_type=jnp.float32
    )


def shift_down(values, amount, fill):
    rows = lax.broadcasted_iota(jnp.int32, values.shape, 0)
    return jnp.where(rows < amount, fill, pltpu.roll(values, amount, 0))


def shift_up(values, amount, fill):
    rows = lax.broadcasted_iota(jnp.int32, values.shape, 0)
    return jnp.where(
        rows >= SUB - amount, fill, pltpu.roll(values, SUB - amount, 0)
    )


def forward_scan_kernel(span_len, pre_input, pre_forget, floor, link, products, partial):
    tiles = span_len // SUB
    scale = jnp.exp(floor[...].astype(jnp.float32))
    width = pre_input.shape[1]
    groups = pre_input.shape[0] // span_len

    def group(g, _):
        def tile(i, carry):
            prod_in, state_in = carry
            rows = pl.ds(pl.multiple_of(g * span_len + i * SUB, SUB), SUB)
            value = pre_input[rows, :]
            leak = scale * jax.nn.sigmoid(-pre_forget[rows, :])
            decay = (1.0 - leak) * link[rows, :1]
            state = leak * value * jax.nn.sigmoid(value)
            for step in (1, 2, 4):
                state = decay * shift_down(state, step, 0.0) + state
                decay = decay * shift_down(decay, step, 1.0)
            state = decay * state_in + state
            decay = decay * prod_in
            products[rows, :] = decay
            partial[rows, :] = state
            return decay[SUB - 1 :, :], state[SUB - 1 :, :]

        lax.fori_loop(
            0, tiles, tile, (jnp.ones((1, width), jnp.float32), jnp.zeros((1, width), jnp.float32))
        )
        return 0

    lax.fori_loop(0, groups, group, 0)


def backward_scan_kernel(span_len, grad_states, pre_forget, floor, link, local, carry_mult, head):
    tiles = span_len // SUB
    scale = jnp.exp(floor[...].astype(jnp.float32))
    width = grad_states.shape[1]
    groups = grad_states.shape[0] // span_len

    def group(g, _):
        def tile(k, carry):
            prod_in, pass_in = carry
            i = tiles - 1 - k
            rows = pl.ds(pl.multiple_of(g * span_len + i * SUB, SUB), SUB)
            upstream = grad_states[rows, :]
            decay = (1.0 - scale * jax.nn.sigmoid(-pre_forget[rows, :])) * link[rows, :1]
            passed = decay * upstream
            for step in (1, 2, 4):
                passed = decay * shift_up(passed, step, 0.0) + passed
                decay = decay * shift_up(decay, step, 1.0)
            passed = decay * pass_in + passed
            decay = decay * prod_in
            local[rows, :] = upstream + shift_up(passed, 1, pass_in)
            carry_mult[rows, :] = shift_up(decay, 1, prod_in)
            return decay[:1, :], passed[:1, :]

        prod_out, pass_out = lax.fori_loop(
            0, tiles, tile, (jnp.ones((1, width), jnp.float32), jnp.zeros((1, width), jnp.float32))
        )
        head[pl.ds(g, 1), :] = pass_out
        return 0

    lax.fori_loop(0, groups, group, 0)


def scan_block(width):
    return 256 if width % 256 == 0 else width


def forward_scan(pre_all, floor, link, span_len, width):
    rows = pre_all.shape[0]
    block = scan_block(width)
    steps = width // block
    out = jax.ShapeDtypeStruct((rows, width), jnp.float32)
    return pl.pallas_call(
        lambda *refs: forward_scan_kernel(span_len, *refs),
        grid=(steps,),
        in_specs=[
            pl.BlockSpec((rows, block), lambda j: (0, j)),
            pl.BlockSpec((rows, block), lambda j: (0, j + steps)),
            pl.BlockSpec((1, block), lambda j: (0, j)),
            pl.BlockSpec((rows, LANES), lambda j: (0, 0)),
        ],
        out_specs=[pl.BlockSpec((rows, block), lambda j: (0, j))] * 2,
        out_shape=[out, out],
    )(pre_all, pre_all, floor, link)


def backward_scan(grad_states, pre_all, floor, link, span_len, width):
    rows = pre_all.shape[0]
    groups = rows // span_len
    block = scan_block(width)
    steps = width // block
    out = jax.ShapeDtypeStruct((rows, width), jnp.float32)
    return pl.pallas_call(
        lambda *refs: backward_scan_kernel(span_len, *refs),
        grid=(steps,),
        in_specs=[
            pl.BlockSpec((rows, block), lambda j: (0, j)),
            pl.BlockSpec((rows, block), lambda j: (0, j + steps)),
            pl.BlockSpec((1, block), lambda j: (0, j)),
            pl.BlockSpec((rows, LANES), lambda j: (0, 0)),
        ],
        out_specs=[pl.BlockSpec((rows, block), lambda j: (0, j))] * 2
        + [pl.BlockSpec((groups, block), lambda j: (0, j))],
        out_shape=[out, out, jax.ShapeDtypeStruct((groups, width), jnp.float32)],
    )(grad_states, pre_all, floor, link)


def entering_forward(mult, value):
    parts, place = lax.axis_size("seq"), lax.axis_index("seq")
    both = lax.all_gather(jnp.stack([mult, value]).astype(jnp.bfloat16), "seq").astype(jnp.float32)
    total = jnp.zeros_like(value)
    for k in range(parts - 1):
        total = jnp.where(k < place, both[k, 0] * total + both[k, 1], total)
    return total


def entering_backward(mult, value):
    parts, place = lax.axis_size("seq"), lax.axis_index("seq")
    both = lax.all_gather(jnp.stack([mult, value]).astype(jnp.bfloat16), "seq").astype(jnp.float32)
    total = jnp.zeros_like(value)
    for k in range(parts - 1, 0, -1):
        total = jnp.where(k > place, both[k, 0] * total + both[k, 1], total)
    return total


def split_mesh(dp, seq):
    side = max(d for d in range(1, dp + 1) if dp % d == 0 and d * d <= dp)
    return dp // side, side, seq // 2


def locate(dims):
    Y, X, Z = dims
    dp, seq = lax.axis_index("dp"), lax.axis_index("seq")
    return lax.div(dp, X), lax.rem(dp, X), lax.div(seq, 2), lax.rem(seq, 2)


def device(dims, y, x, z, c):
    return (y * dims[1] + x, z * 2 + c)


def hop(place, k, size):
    return lax.rem(place + k, size)


def greet(dims, here):
    Y, X, Z = dims
    y, x, z, c = here
    barrier = pltpu.get_barrier_semaphore()
    peers = [device(dims, y, x, z, 1 - c)]
    peers += [device(dims, hop(y, k, Y), x, z, c) for k in range(1, Y)]
    peers += [device(dims, y, hop(x, k, X), z, c) for k in range(1, X)]
    peers += [device(dims, y, x, hop(z, k, Z), c) for k in range(1, Z)]
    for peer in peers:
        pl.semaphore_signal(barrier, inc=1, device_id=peer, device_id_type=MESH)
    pl.semaphore_wait(barrier, len(peers))


def scatter_kernel(dims, depth, wide, pairs, spans, has_vec, *refs):
    Y, X, Z = dims
    half = wide // 2
    f32, low = jnp.float32, jnp.bfloat16
    refs = list(refs)
    take = lambda n: [refs.pop(0) for _ in range(n)]
    lefts, rights = take(pairs), take(pairs)
    vec = take(1)[0] if has_vec else None
    outs = take(len(spans))
    (part, core_in, one_a, one_b, in_a, in_b, two_a, two_b, far_a, far_b, three, line_in) = take(12)
    (core_s, core_r, ya_s, ya_r, xb_s, xb_r, xa_s, xa_r, yb_s, yb_r, z_s, z_r) = take(12)
    (core_f, ya_f, xb_f, xa_f, yb_f, z_f) = take(6)
    here = locate(dims)
    y, x, z, c = here
    greet(dims, here)
    total = spans[-1][2]

    def send(src, dst, ss, rs, peer):
        return pltpu.make_async_remote_copy(
            src_ref=src, dst_ref=dst, send_sem=ss, recv_sem=rs, device_id=peer, device_id_type=MESH
        )

    def core_copies(t):
        s = lax.rem(t, SLOTS)
        return [
            (
                send(part.at[s, 1 - c], core_in.at[s], core_s.at[s], core_r.at[s],
                     device(dims, y, x, z, 1 - c)),
                core_f.at[0],
                device(dims, y, x, z, 1 - c),
            )
        ]

    def first_copies(t):
        s = lax.rem(t, SLOTS)
        out = []
        for k in range(1, Y):
            to, frm = hop(y, k, Y), hop(y, Y - k, Y)
            out.append(
                (
                    send(one_a.at[s, to], in_a.at[s, k - 1], ya_s.at[s, k - 1], ya_r.at[s, k - 1],
                         device(dims, to, x, z, c)),
                    ya_f.at[k - 1],
                    device(dims, frm, x, z, c),
                )
            )
        for k in range(1, X):
            to, frm = hop(x, k, X), hop(x, X - k, X)
            out.append(
                (
                    send(one_b.at[s, to], in_b.at[s, k - 1], xb_s.at[s, k - 1], xb_r.at[s, k - 1],
                         device(dims, y, to, z, c)),
                    xb_f.at[k - 1],
                    device(dims, y, frm, z, c),
                )
            )
        return out

    def second_copies(t):
        s = lax.rem(t, SLOTS)
        out = []
        for k in range(1, X):
            to, frm = hop(x, k, X), hop(x, X - k, X)
            out.append(
                (
                    send(two_a.at[s, to], far_a.at[s, k - 1], xa_s.at[s, k - 1], xa_r.at[s, k - 1],
                         device(dims, y, to, z, c)),
                    xa_f.at[k - 1],
                    device(dims, y, frm, z, c),
                )
            )
        for k in range(1, Y):
            to, frm = hop(y, k, Y), hop(y, Y - k, Y)
            out.append(
                (
                    send(two_b.at[s, to], far_b.at[s, k - 1], yb_s.at[s, k - 1], yb_r.at[s, k - 1],
                         device(dims, to, x, z, c)),
                    yb_f.at[k - 1],
                    device(dims, frm, x, z, c),
                )
            )
        return out

    def line_copies(t):
        s = lax.rem(t, SLOTS)
        out = []
        for k in range(1, Z):
            to, frm = hop(z, k, Z), hop(z, Z - k, Z)
            out.append(
                (
                    send(three.at[s, to], line_in.at[s, k - 1], z_s.at[s, k - 1], z_r.at[s, k - 1],
                         device(dims, y, x, to, c)),
                    z_f.at[k - 1],
                    device(dims, y, x, frm, c),
                )
            )
        return out

    def begin(copies, t):
        for copy, free, _ in copies:

            @pl.when(t >= SLOTS)
            def _():
                pl.semaphore_wait(free, 1)

            copy.start()

    def arrive(copies):
        for copy, _, _ in copies:
            copy.wait()

    def release(copies, t):
        for _, free, giver in copies:

            @pl.when(t + SLOTS < total)
            def _():
                pl.semaphore_signal(free, inc=1, device_id=giver, device_id_type=MESH)

    def produce(t):
        s = lax.rem(t, SLOTS)
        for pair in range(pairs):
            low_t, high_t = rights_span[pair]

            @pl.when(jnp.logical_and(t >= low_t, t < high_t))
            def _():
                columns = pl.ds(pl.multiple_of((t - low_t) * wide, wide), wide)

                def block(i, _):
                    rows = Z * 2 * depth
                    first = pl.multiple_of(i * rows, rows)
                    value = jnp.dot(
                        lefts[pair][pl.ds(first, rows), :],
                        rights[pair][:, columns],
                        preferred_element_type=f32,
                    ).astype(low)
                    value = value.reshape(Z, 2, depth, wide)
                    for core in range(2):
                        part[s, core, lax.div(i, X), lax.rem(i, X)] = value[:, core]
                    return 0

                lax.fori_loop(0, Y * X, block, 0)

        if has_vec:

            @pl.when(t == total - 1)
            def _():
                def block(i, _):
                    rows = Z * 2 * depth
                    first = pl.multiple_of(i * rows, rows)
                    value = vec[pl.ds(first, rows), :].reshape(Z, 2, depth, vec.shape[1])
                    for core in range(2):
                        part[s, core, lax.div(i, X), lax.rem(i, X), :, :, : vec.shape[1]] = value[
                            :, core
                        ]
                    return 0

                lax.fori_loop(0, Y * X, block, 0)

    rights_span = []
    start = 0
    for pair in range(pairs):
        count = rights[pair].shape[1] // wide
        rights_span.append((start, start + count))
        start += count

    def step(t, _):
        @pl.when(t < total)
        def _():
            produce(t)
            begin(core_copies(t), t)

        u = t - 1

        @pl.when(jnp.logical_and(u >= 0, u < total))
        def _():
            s = lax.rem(u, SLOTS)
            copies = core_copies(u)
            arrive(copies)

            def block(i, _):
                i, j = lax.div(i, X), lax.rem(i, X)
                value = part[s, c, i, j].astype(f32) + core_in[s, i, j].astype(f32)
                value = value.astype(low)
                one_a[s, i, j] = value[:, :, :half]
                one_b[s, j, i] = value[:, :, half:]
                return 0

            lax.fori_loop(0, Y * X, block, 0)
            release(copies, u)
            begin(first_copies(u), u)

        v = t - 2

        @pl.when(jnp.logical_and(v >= 0, v < total))
        def _():
            s = lax.rem(v, SLOTS)
            copies = first_copies(v)
            arrive(copies)
            value = one_a[s, y].astype(f32)
            for k in range(Y - 1):
                value = value + in_a[s, k].astype(f32)
            two_a[s] = value.astype(low)
            value = one_b[s, x].astype(f32)
            for k in range(X - 1):
                value = value + in_b[s, k].astype(f32)
            two_b[s] = value.astype(low)
            release(copies, v)
            begin(second_copies(v), v)

        w = t - 3

        @pl.when(jnp.logical_and(w >= 0, w < total))
        def _():
            s = lax.rem(w, SLOTS)
            copies = second_copies(w)
            arrive(copies)
            value = two_a[s, x].astype(f32)
            for k in range(X - 1):
                value = value + far_a[s, k].astype(f32)
            three[s, :, :, :half] = value.astype(low)
            value = two_b[s, y].astype(f32)
            for k in range(Y - 1):
                value = value + far_b[s, k].astype(f32)
            three[s, :, :, half:] = value.astype(low)
            release(copies, w)
            begin(line_copies(w), w)

        q = t - 4

        @pl.when(q >= 0)
        def _():
            s = lax.rem(q, SLOTS)
            copies = line_copies(q)
            arrive(copies)
            value = three[s, z].astype(f32)
            for k in range(Z - 1):
                value = value + line_in[s, k].astype(f32)
            release(copies, q)
            for index, (_, low_t, high_t) in enumerate(spans):

                @pl.when(jnp.logical_and(q >= low_t, q < high_t))
                def _():
                    outs[index][:, pl.ds(pl.multiple_of((q - low_t) * wide, wide), wide)] = value

        return 0

    lax.fori_loop(0, total + 4, step, 0)


def scatter_call(dims, depth, wide, pairs, widths, vec, collective_id):
    Y, X, Z = dims
    half = wide // 2
    low = jnp.bfloat16
    widths = list(widths)
    if vec is not None:
        widths.append(wide)
    spans, start = [], 0
    for n in widths:
        spans.append((n, start, start + n // wide))
        start += n // wide
    operands = [a for a, _ in pairs] + [b for _, b in pairs] + ([vec] if vec is not None else [])
    vmem = lambda *shape: pltpu.VMEM((SLOTS,) + shape, low)
    dma = lambda *shape: pltpu.SemaphoreType.DMA((SLOTS,) + shape)
    reg = lambda n: pltpu.SemaphoreType.REGULAR((n,))
    y1, x1, z1 = max(Y - 1, 1), max(X - 1, 1), max(Z - 1, 1)
    scratch = [
        vmem(2, Y, X, Z, depth, wide),
        vmem(Y, X, Z, depth, wide),
        vmem(Y, X, Z, depth, half),
        vmem(X, Y, Z, depth, half),
        vmem(y1, X, Z, depth, half),
        vmem(x1, Y, Z, depth, half),
        vmem(X, Z, depth, half),
        vmem(Y, Z, depth, half),
        vmem(x1, Z, depth, half),
        vmem(y1, Z, depth, half),
        vmem(Z, depth, wide),
        vmem(z1, depth, wide),
    ]
    scratch += [dma(), dma()]
    scratch += [dma(y1), dma(y1), dma(x1), dma(x1), dma(x1), dma(x1), dma(y1), dma(y1), dma(z1), dma(z1)]
    scratch += [reg(1), reg(y1), reg(x1), reg(x1), reg(y1), reg(z1)]
    return pl.pallas_call(
        functools.partial(
            scatter_kernel, dims, depth, wide, len(pairs), spans, vec is not None
        ),
        out_shape=[jax.ShapeDtypeStruct((depth, n), jnp.float32) for n in widths],
        in_specs=[pl.BlockSpec(memory_space=pltpu.VMEM)] * len(operands),
        out_specs=[pl.BlockSpec(memory_space=pltpu.VMEM)] * len(widths),
        scratch_shapes=scratch,
        compiler_params=pltpu.CompilerParams(
            collective_id=collective_id, has_side_effects=True, vmem_limit_bytes=60 * 2**20
        ),
    )(*operands)


def gather_all(shard):
    return lax.all_gather(shard, ALL, axis=0, tiled=True)


def scatter_all(whole):
    return lax.psum_scatter(whole, ALL, scatter_dimension=0, tiled=True)


def shards(
    inputs,
    segment_ids,
    cotangent,
    mixer_gain,
    input_proj,
    forget_proj,
    gate_proj,
    floor_log,
    output_gain,
    output_proj,
    dense_gain,
    up_first,
    up_second,
    down_proj,
):
    width = inputs.shape[-1]
    hidden = up_first.shape[1]
    groups = inputs.shape[0] * inputs.shape[1]
    span_len = inputs.shape[2]
    rows_all = groups * span_len
    parts, place = lax.axis_size("seq"), lax.axis_index("seq")

    vectors = jnp.stack([mixer_gain, floor_log, output_gain, dense_gain], axis=1)
    vectors = jnp.pad(vectors, ((0, 0), (0, LANES - 4)))
    mix_full = gather_all(
        jnp.concatenate([input_proj, forget_proj, gate_proj, vectors], axis=1)
    )
    out_full = gather_all(output_proj)
    up_full = gather_all(jnp.concatenate([up_first, up_second], axis=1))
    down_full = gather_all(down_proj)
    gains = mix_full[:, 3 * width : 3 * width + 4].T
    mixer_gain_all = gains[0:1].astype(jnp.float32)
    floor_all = gains[1:2].astype(jnp.float32)
    out_gain_all = gains[2:3].astype(jnp.float32)
    dense_gain_all = gains[3:4].astype(jnp.float32)

    seg = segment_ids.reshape(groups, span_len)
    before = lax.ppermute(seg[:, -1:], "seq", [(i, i + 1) for i in range(parts - 1)])
    before = jnp.where(place == 0, -1, before)
    link = (seg == jnp.concatenate([before, seg[:, :-1]], axis=1)).astype(jnp.float32)
    link = jnp.broadcast_to(link.reshape(rows_all, 1), (rows_all, LANES))

    flat = inputs.reshape(rows_all, width)
    scale_one = lax.rsqrt(jnp.mean(flat * flat, axis=1, keepdims=True) + norm_eps)
    scaled_one = flat * scale_one
    normed_one = (scaled_one * mixer_gain_all).astype(jnp.bfloat16)
    pre_all = dot(normed_one, mix_full)
    pre_input = pre_all[:, :width]
    pre_forget = pre_all[:, width : 2 * width]
    pre_gate = pre_all[:, 2 * width : 3 * width]

    products, partial_state = forward_scan(pre_all, floor_all, link, span_len, width)
    products = products.reshape(groups, span_len, width)
    span_mult = products[:, -1]
    entering = entering_forward(
        span_mult, partial_state.reshape(groups, span_len, width)[:, -1]
    )
    states = products * entering[:, None, :] + partial_state.reshape(groups, span_len, width)
    states_flat = states.reshape(rows_all, width)
    state_scale = lax.rsqrt(jnp.mean(states_flat * states_flat, axis=1, keepdims=True) + norm_eps)
    normed_state = states_flat * state_scale
    gate_out = jax.nn.silu(pre_gate)
    mixed = (normed_state * out_gain_all * gate_out).astype(jnp.bfloat16)
    middle = flat + dot(mixed, out_full)
    scale_two = lax.rsqrt(jnp.mean(middle * middle, axis=1, keepdims=True) + norm_eps)
    scaled_two = middle * scale_two
    normed_two = (scaled_two * dense_gain_all).astype(jnp.bfloat16)
    up_both = dot(normed_two, up_full)
    up_one, up_two = up_both[:, :hidden], up_both[:, hidden:]
    activated = (jax.nn.silu(up_one) * up_two).astype(jnp.bfloat16)
    block_out = (middle + dot(activated, down_full)).reshape(inputs.shape)

    grad_flat = cotangent.reshape(rows_all, width)
    grad_dense = grad_flat.astype(jnp.bfloat16)
    grad_act = contract_last(grad_dense, down_full)
    grad_up = jnp.concatenate(
        [
            (grad_act * up_two * silu_slope(up_one)).astype(jnp.bfloat16),
            (grad_act * jax.nn.silu(up_one)).astype(jnp.bfloat16),
        ],
        axis=1,
    )
    grad_normed_two = contract_last(grad_up, up_full)
    gain_two = jnp.sum(grad_normed_two * scaled_two, axis=0)
    grad_middle = grad_flat + norm_back(grad_normed_two * dense_gain_all, scaled_two, scale_two)
    grad_mixer = grad_middle.astype(jnp.bfloat16)
    grad_mix_in = contract_last(grad_mixer, out_full)
    gain_out = jnp.sum(grad_mix_in * normed_state * gate_out, axis=0)
    grad_pre_gate = (
        grad_mix_in * normed_state * out_gain_all * silu_slope(pre_gate)
    ).astype(jnp.bfloat16)
    grad_states = norm_back(grad_mix_in * out_gain_all * gate_out, normed_state, state_scale)

    local_grad, carry_mult, head_grad = backward_scan(
        grad_states, pre_all, floor_all, link, span_len, width
    )
    arriving = entering_backward(span_mult, head_grad)
    adjoint = (
        local_grad.reshape(groups, span_len, width)
        + carry_mult.reshape(groups, span_len, width) * arriving[:, None, :]
    ).reshape(rows_all, width)
    previous = jnp.concatenate([entering[:, None, :], states[:, :-1]], axis=1)
    previous = previous.reshape(rows_all, width) * link[:, :1]
    leak = jnp.exp(floor_all) * jax.nn.sigmoid(-pre_forget)
    grad_forget = adjoint * (previous - jax.nn.silu(pre_input))
    grad_pre_input = (adjoint * leak * silu_slope(pre_input)).astype(jnp.bfloat16)
    grad_pre_forget = (grad_forget * leak * jax.nn.sigmoid(pre_forget)).astype(jnp.bfloat16)
    floor_sum = -jnp.sum(grad_forget * leak, axis=0)
    grad_pre = jnp.concatenate(
        [
            grad_pre_input,
            grad_pre_forget,
            grad_pre_gate,
            jnp.zeros((rows_all, LANES), jnp.bfloat16),
        ],
        axis=1,
    )
    block_all = contract_last(grad_pre, mix_full)
    gain_one = jnp.sum(block_all * scaled_one, axis=0)
    input_grad = (
        grad_middle + norm_back(block_all * mixer_gain_all, scaled_one, scale_one)
    ).reshape(inputs.shape)

    low = jnp.bfloat16
    vector_sums = jnp.stack([gain_one, floor_sum, gain_out, gain_two], axis=1)
    vector_sums = jnp.pad(vector_sums, ((0, 0), (0, LANES - 4))).astype(low)
    depth, deep = output_proj.shape[0], down_proj.shape[0]
    wide, narrow = 512, 256
    own_kernel = (
        depth % 16 == 0
        and deep % 16 == 0
        and parts % 2 == 0
        and width % wide == 0
        and hidden % wide == 0
    )
    if own_kernel:
        dims = split_mesh(lax.axis_size("dp"), parts)
        *grads, vector_terms = scatter_call(
            dims,
            depth,
            wide,
            [(normed_one.T, grad_pre), (mixed.T, grad_mixer), (normed_two.T, grad_up)],
            [width] * 4 + [hidden] * 2,
            vector_sums,
            1,
        )
        (down_grad,) = scatter_call(
            dims, deep, narrow, [(activated.T, grad_dense)], [width], None, 2
        )
    else:
        terms = scatter_all(
            jnp.concatenate(
                [
                    contract_rows(normed_one, grad_pre[:, : 3 * width]).astype(low),
                    contract_rows(mixed, grad_mixer).astype(low),
                    contract_rows(normed_two, grad_up).astype(low),
                    vector_sums,
                ],
                axis=1,
            )
        ).astype(jnp.float32)
        marks = [width, 2 * width, 3 * width, 4 * width]
        marks += [4 * width + hidden, 4 * width + 2 * hidden]
        *grads, vector_terms = jnp.split(terms, marks, axis=1)
        down_grad = scatter_all(contract_rows(activated, grad_dense).astype(low))
        down_grad = down_grad.astype(jnp.float32)
    return (
        block_out,
        input_grad,
        vector_terms[:, 0],
        grads[0],
        grads[1],
        grads[2],
        vector_terms[:, 1],
        vector_terms[:, 2],
        grads[3],
        vector_terms[:, 3],
        grads[4],
        grads[5],
        down_grad,
    )


def solution(mesh):
    whole = P(None, "dp", "seq", None)
    vector = P(ALL)
    matrix = P(ALL, None)
    return jax.shard_map(
        shards,
        mesh=mesh,
        in_specs=(
            whole,
            P(None, "dp", "seq"),
            whole,
            vector,
            matrix,
            matrix,
            matrix,
            vector,
            vector,
            matrix,
            vector,
            matrix,
            matrix,
            matrix,
        ),
        out_specs=(
            whole,
            whole,
            vector,
            matrix,
            matrix,
            matrix,
            vector,
            vector,
            matrix,
            vector,
            matrix,
            matrix,
            matrix,
        ),
        check_vma=False,
    )
```

```python
import functools

import jax
import jax.numpy as jnp
from jax import lax
from jax.experimental import pallas as pl
from jax.experimental.pallas import tpu as pltpu
from jax.sharding import PartitionSpec as P

norm_eps = 1e-06
ALL = ("dp", "seq")
LANES = 128
SUB = 8
MESH = pl.DeviceIdType.MESH
SLOTS = 2
AHEAD = 12
EXTRA = 256


def silu_slope(values):
    logistic = jax.nn.sigmoid(values)
    return logistic * (1.0 + values * (1.0 - logistic))


def norm_back(upstream, scaled, factor):
    return factor * (upstream - scaled * jnp.mean(upstream * scaled, axis=-1, keepdims=True))


def dot(left, right):
    return jnp.dot(left, right, preferred_element_type=jnp.float32)


def contract_last(left, right):
    return lax.dot_general(
        left, right, (((1,), (1,)), ((), ())), preferred_element_type=jnp.float32
    )


def contract_rows(left, right):
    return lax.dot_general(
        left, right, (((0,), (0,)), ((), ())), preferred_element_type=jnp.float32
    )


def shift_down(values, amount, fill):
    rows = lax.broadcasted_iota(jnp.int32, values.shape, 0)
    return jnp.where(rows < amount, fill, pltpu.roll(values, amount, 0))


def shift_up(values, amount, fill):
    rows = lax.broadcasted_iota(jnp.int32, values.shape, 0)
    return jnp.where(
        rows >= SUB - amount, fill, pltpu.roll(values, SUB - amount, 0)
    )


def forward_scan_kernel(span_len, pre_input, pre_forget, floor, link, products, partial):
    tiles = span_len // SUB
    scale = jnp.exp(floor[...].astype(jnp.float32))
    width = pre_input.shape[1]
    groups = pre_input.shape[0] // span_len

    def tile(i, carries):
        out = []
        for g in range(groups):
            prod_in, state_in = carries[g]
            rows = pl.ds(pl.multiple_of(g * span_len + i * SUB, SUB), SUB)
            value = pre_input[rows, :]
            leak = scale * jax.nn.sigmoid(-pre_forget[rows, :])
            decay = (1.0 - leak) * link[rows, :1]
            state = leak * value * jax.nn.sigmoid(value)
            for step in (1, 2, 4):
                state = decay * shift_down(state, step, 0.0) + state
                decay = decay * shift_down(decay, step, 1.0)
            state = decay * state_in + state
            decay = decay * prod_in
            products[rows, :] = decay
            partial[rows, :] = state
            out.append((decay[SUB - 1 :, :], state[SUB - 1 :, :]))
        return tuple(out)

    start = (jnp.ones((1, width), jnp.float32), jnp.zeros((1, width), jnp.float32))
    lax.fori_loop(0, tiles, tile, (start,) * groups)


def backward_scan_kernel(span_len, grad_states, pre_forget, floor, link, local, carry_mult, head):
    tiles = span_len // SUB
    scale = jnp.exp(floor[...].astype(jnp.float32))
    width = grad_states.shape[1]
    groups = grad_states.shape[0] // span_len

    def tile(k, carries):
        i = tiles - 1 - k
        out = []
        for g in range(groups):
            prod_in, pass_in = carries[g]
            rows = pl.ds(pl.multiple_of(g * span_len + i * SUB, SUB), SUB)
            upstream = grad_states[rows, :]
            decay = (1.0 - scale * jax.nn.sigmoid(-pre_forget[rows, :])) * link[rows, :1]
            passed = decay * upstream
            for step in (1, 2, 4):
                passed = decay * shift_up(passed, step, 0.0) + passed
                decay = decay * shift_up(decay, step, 1.0)
            passed = decay * pass_in + passed
            decay = decay * prod_in
            local[rows, :] = upstream + shift_up(passed, 1, pass_in)
            carry_mult[rows, :] = shift_up(decay, 1, prod_in)
            out.append((decay[:1, :], passed[:1, :]))
        return tuple(out)

    start = (jnp.ones((1, width), jnp.float32), jnp.zeros((1, width), jnp.float32))
    ends = lax.fori_loop(0, tiles, tile, (start,) * groups)
    for g in range(groups):
        head[g : g + 1, :] = ends[g][1]


def scan_block(width):
    return 512 if width % 512 == 0 else width


def forward_scan(pre_all, floor, link, span_len, width):
    rows = pre_all.shape[0]
    block = scan_block(width)
    steps = width // block
    out = jax.ShapeDtypeStruct((rows, width), jnp.float32)
    return pl.pallas_call(
        lambda *refs: forward_scan_kernel(span_len, *refs),
        grid=(steps,),
        in_specs=[
            pl.BlockSpec((rows, block), lambda j: (0, j)),
            pl.BlockSpec((rows, block), lambda j: (0, j + steps)),
            pl.BlockSpec((1, block), lambda j: (0, j)),
            pl.BlockSpec((rows, LANES), lambda j: (0, 0)),
        ],
        out_specs=[pl.BlockSpec((rows, block), lambda j: (0, j))] * 2,
        out_shape=[out, out],
    )(pre_all, pre_all, floor, link)


def backward_scan(grad_states, pre_all, floor, link, span_len, width):
    rows = pre_all.shape[0]
    groups = rows // span_len
    block = scan_block(width)
    steps = width // block
    out = jax.ShapeDtypeStruct((rows, width), jnp.float32)
    return pl.pallas_call(
        lambda *refs: backward_scan_kernel(span_len, *refs),
        grid=(steps,),
        in_specs=[
            pl.BlockSpec((rows, block), lambda j: (0, j)),
            pl.BlockSpec((rows, block), lambda j: (0, j + steps)),
            pl.BlockSpec((1, block), lambda j: (0, j)),
            pl.BlockSpec((rows, LANES), lambda j: (0, 0)),
        ],
        out_specs=[pl.BlockSpec((rows, block), lambda j: (0, j))] * 2
        + [pl.BlockSpec((groups, block), lambda j: (0, j))],
        out_shape=[out, out, jax.ShapeDtypeStruct((groups, width), jnp.float32)],
    )(grad_states, pre_all, floor, link)


def exchange(value):
    return lax.all_gather(value.astype(jnp.bfloat16), "seq").astype(jnp.float32)


def entering_forward(mults, values):
    parts, place = lax.axis_size("seq"), lax.axis_index("seq")
    total = jnp.zeros_like(values[0])
    for k in range(parts - 1):
        total = jnp.where(k < place, mults[k] * total + values[k], total)
    return total


def entering_backward(mults, values):
    parts, place = lax.axis_size("seq"), lax.axis_index("seq")
    total = jnp.zeros_like(values[0])
    for k in range(parts - 1, 0, -1):
        total = jnp.where(k > place, mults[k] * total + values[k], total)
    return total


def split_mesh(dp, seq):
    side = max(d for d in range(1, dp + 1) if dp % d == 0 and d * d <= dp)
    return dp // side, side, seq // 2


def locate(dims):
    Y, X, Z = dims
    dp, seq = lax.axis_index("dp"), lax.axis_index("seq")
    return lax.div(dp, X), lax.rem(dp, X), lax.div(seq, 2), lax.rem(seq, 2)


def device(dims, y, x, z, c):
    return (y * dims[1] + x, z * 2 + c)


def hop(place, k, size):
    return lax.rem(place + k, size)


def greet(dims, here):
    Y, X, Z = dims
    y, x, z, c = here
    barrier = pltpu.get_barrier_semaphore()
    peers = [device(dims, y, x, z, 1 - c)]
    peers += [device(dims, hop(y, k, Y), x, z, c) for k in range(1, Y)]
    peers += [device(dims, y, hop(x, k, X), z, c) for k in range(1, X)]
    peers += [device(dims, y, x, hop(z, k, Z), c) for k in range(1, Z)]
    for peer in peers:
        pl.semaphore_signal(barrier, inc=1, device_id=peer, device_id_type=MESH)
    pl.semaphore_wait(barrier, len(peers))


def scatter_kernel(dims, depth, wide, pairs, spans, has_vec, *refs):
    Y, X, Z = dims
    half = wide // 2
    f32, low = jnp.float32, jnp.bfloat16
    refs = list(refs)
    take = lambda n: [refs.pop(0) for _ in range(n)]
    lefts, rights = take(pairs), take(pairs)
    vec = take(1)[0] if has_vec else None
    outs = take(len(spans))
    (part, core_in, one_a, one_b, in_a, in_b, two_a, two_b, far_a, far_b, three, line_in) = take(12)
    (core_s, core_r, ya_s, ya_r, xb_s, xb_r, xa_s, xa_r, yb_s, yb_r, z_s, z_r) = take(12)
    (core_f, ya_f, xb_f, xa_f, yb_f, z_f) = take(6)
    here = locate(dims)
    y, x, z, c = here
    greet(dims, here)
    total = spans[-1][2]

    def send(src, dst, ss, rs, peer):
        return pltpu.make_async_remote_copy(
            src_ref=src, dst_ref=dst, send_sem=ss, recv_sem=rs, device_id=peer, device_id_type=MESH
        )

    def core_copies(t):
        s = lax.rem(t, SLOTS)
        return [
            (
                send(part.at[s, 1 - c], core_in.at[s], core_s.at[s], core_r.at[s],
                     device(dims, y, x, z, 1 - c)),
                core_f.at[0],
                device(dims, y, x, z, 1 - c),
            )
        ]

    def first_copies(t):
        s = lax.rem(t, SLOTS)
        out = []
        for k in range(1, Y):
            to, frm = hop(y, k, Y), hop(y, Y - k, Y)
            out.append(
                (
                    send(one_a.at[s, to], in_a.at[s, k - 1], ya_s.at[s, k - 1], ya_r.at[s, k - 1],
                         device(dims, to, x, z, c)),
                    ya_f.at[k - 1],
                    device(dims, frm, x, z, c),
                )
            )
        for k in range(1, X):
            to, frm = hop(x, k, X), hop(x, X - k, X)
            out.append(
                (
                    send(one_b.at[s, to], in_b.at[s, k - 1], xb_s.at[s, k - 1], xb_r.at[s, k - 1],
                         device(dims, y, to, z, c)),
                    xb_f.at[k - 1],
                    device(dims, y, frm, z, c),
                )
            )
        return out

    def second_copies(t):
        s = lax.rem(t, SLOTS)
        out = []
        for k in range(1, X):
            to, frm = hop(x, k, X), hop(x, X - k, X)
            out.append(
                (
                    send(two_a.at[s, to], far_a.at[s, k - 1], xa_s.at[s, k - 1], xa_r.at[s, k - 1],
                         device(dims, y, to, z, c)),
                    xa_f.at[k - 1],
                    device(dims, y, frm, z, c),
                )
            )
        for k in range(1, Y):
            to, frm = hop(y, k, Y), hop(y, Y - k, Y)
            out.append(
                (
                    send(two_b.at[s, to], far_b.at[s, k - 1], yb_s.at[s, k - 1], yb_r.at[s, k - 1],
                         device(dims, to, x, z, c)),
                    yb_f.at[k - 1],
                    device(dims, frm, x, z, c),
                )
            )
        return out

    def line_copies(t):
        s = lax.rem(t, SLOTS)
        out = []
        for k in range(1, Z):
            to, frm = hop(z, k, Z), hop(z, Z - k, Z)
            out.append(
                (
                    send(three.at[s, to], line_in.at[s, k - 1], z_s.at[s, k - 1], z_r.at[s, k - 1],
                         device(dims, y, x, to, c)),
                    z_f.at[k - 1],
                    device(dims, y, x, frm, c),
                )
            )
        return out

    def begin(copies, t):
        for copy, free, _ in copies:

            @pl.when(t >= SLOTS)
            def _():
                pl.semaphore_wait(free, 1)

            copy.start()

    def arrive(copies):
        for copy, _, _ in copies:
            copy.wait()

    def release(copies, t):
        for _, free, giver in copies:

            @pl.when(t + SLOTS < total)
            def _():
                pl.semaphore_signal(free, inc=1, device_id=giver, device_id_type=MESH)

    def produce(t):
        s = lax.rem(t, SLOTS)
        for pair in range(pairs):
            low_t, high_t = rights_span[pair]

            @pl.when(jnp.logical_and(t >= low_t, t < high_t))
            def _():
                columns = pl.ds(pl.multiple_of((t - low_t) * wide, wide), wide)

                def block(i, _):
                    rows = Z * 2 * depth
                    first = pl.multiple_of(i * rows, rows)
                    value = jnp.dot(
                        lefts[pair][pl.ds(first, rows), :],
                        rights[pair][:, columns],
                        preferred_element_type=f32,
                    ).astype(low)
                    value = value.reshape(Z, 2, depth, wide)
                    for core in range(2):
                        part[s, core, lax.div(i, X), lax.rem(i, X)] = value[:, core]
                    return 0

                lax.fori_loop(0, Y * X, block, 0)

        if has_vec:

            @pl.when(t == total - 1)
            def _():
                def block(i, _):
                    rows = Z * 2 * depth
                    first = pl.multiple_of(i * rows, rows)
                    value = vec[pl.ds(first, rows), :].reshape(Z, 2, depth, vec.shape[1])
                    for core in range(2):
                        part[s, core, lax.div(i, X), lax.rem(i, X), :, :, : vec.shape[1]] = value[
                            :, core
                        ]
                    return 0

                lax.fori_loop(0, Y * X, block, 0)

    rights_span = []
    start = 0
    for pair in range(pairs):
        count = rights[pair].shape[1] // wide
        rights_span.append((start, start + count))
        start += count

    def step(t, _):
        @pl.when(t < total)
        def _():
            produce(t)
            begin(core_copies(t), t)

        u = t - 1

        @pl.when(jnp.logical_and(u >= 0, u < total))
        def _():
            s = lax.rem(u, SLOTS)
            copies = core_copies(u)
            arrive(copies)

            def block(i, _):
                i, j = lax.div(i, X), lax.rem(i, X)
                value = part[s, c, i, j].astype(f32) + core_in[s, i, j].astype(f32)
                value = value.astype(low)
                one_a[s, i, j] = value[:, :, :half]
                one_b[s, j, i] = value[:, :, half:]
                return 0

            lax.fori_loop(0, Y * X, block, 0)
            release(copies, u)
            begin(first_copies(u), u)

        v = t - 2

        @pl.when(jnp.logical_and(v >= 0, v < total))
        def _():
            s = lax.rem(v, SLOTS)
            copies = first_copies(v)
            arrive(copies)
            value = one_a[s, y].astype(f32)
            for k in range(Y - 1):
                value = value + in_a[s, k].astype(f32)
            two_a[s] = value.astype(low)
            value = one_b[s, x].astype(f32)
            for k in range(X - 1):
                value = value + in_b[s, k].astype(f32)
            two_b[s] = value.astype(low)
            release(copies, v)
            begin(second_copies(v), v)

        w = t - 3

        @pl.when(jnp.logical_and(w >= 0, w < total))
        def _():
            s = lax.rem(w, SLOTS)
            copies = second_copies(w)
            arrive(copies)
            value = two_a[s, x].astype(f32)
            for k in range(X - 1):
                value = value + far_a[s, k].astype(f32)
            three[s, :, :, :half] = value.astype(low)
            value = two_b[s, y].astype(f32)
            for k in range(Y - 1):
                value = value + far_b[s, k].astype(f32)
            three[s, :, :, half:] = value.astype(low)
            release(copies, w)
            begin(line_copies(w), w)

        q = t - 4

        @pl.when(q >= 0)
        def _():
            s = lax.rem(q, SLOTS)
            copies = line_copies(q)
            arrive(copies)
            value = three[s, z].astype(f32)
            for k in range(Z - 1):
                value = value + line_in[s, k].astype(f32)
            release(copies, q)
            for index, (_, low_t, high_t) in enumerate(spans):

                @pl.when(jnp.logical_and(q >= low_t, q < high_t))
                def _():
                    outs[index][:, pl.ds(pl.multiple_of((q - low_t) * wide, wide), wide)] = value

        return 0

    lax.fori_loop(0, total + 4, step, 0)


def scatter_call(dims, depth, wide, pairs, widths, vec, collective_id):
    Y, X, Z = dims
    half = wide // 2
    low = jnp.bfloat16
    widths = list(widths)
    if vec is not None:
        widths.append(wide)
    spans, start = [], 0
    for n in widths:
        spans.append((n, start, start + n // wide))
        start += n // wide
    operands = [a for a, _ in pairs] + [b for _, b in pairs] + ([vec] if vec is not None else [])
    vmem = lambda *shape: pltpu.VMEM((SLOTS,) + shape, low)
    dma = lambda *shape: pltpu.SemaphoreType.DMA((SLOTS,) + shape)
    reg = lambda n: pltpu.SemaphoreType.REGULAR((n,))
    y1, x1, z1 = max(Y - 1, 1), max(X - 1, 1), max(Z - 1, 1)
    scratch = [
        vmem(2, Y, X, Z, depth, wide),
        vmem(Y, X, Z, depth, wide),
        vmem(Y, X, Z, depth, half),
        vmem(X, Y, Z, depth, half),
        vmem(y1, X, Z, depth, half),
        vmem(x1, Y, Z, depth, half),
        vmem(X, Z, depth, half),
        vmem(Y, Z, depth, half),
        vmem(x1, Z, depth, half),
        vmem(y1, Z, depth, half),
        vmem(Z, depth, wide),
        vmem(z1, depth, wide),
    ]
    scratch += [dma(), dma()]
    scratch += [dma(y1), dma(y1), dma(x1), dma(x1), dma(x1), dma(x1), dma(y1), dma(y1), dma(z1), dma(z1)]
    scratch += [reg(1), reg(y1), reg(x1), reg(x1), reg(y1), reg(z1)]
    return pl.pallas_call(
        functools.partial(
            scatter_kernel, dims, depth, wide, len(pairs), spans, vec is not None
        ),
        out_shape=[jax.ShapeDtypeStruct((depth, n), jnp.float32) for n in widths],
        in_specs=[pl.BlockSpec(memory_space=pltpu.VMEM)] * len(operands),
        out_specs=[pl.BlockSpec(memory_space=pltpu.VMEM)] * len(widths),
        scratch_shapes=scratch,
        compiler_params=pltpu.CompilerParams(
            collective_id=collective_id, has_side_effects=True, vmem_limit_bytes=60 * 2**20
        ),
    )(*operands)


def gather_kernel(dims, wides, *refs):
    Y, X, Z = dims
    refs = list(refs)
    take = lambda n: [refs.pop(0) for _ in range(n)]
    n = len(wides)
    shards, wholes = take(n), take(n)
    own_sem, zs, zr, first_s, first_r, next_s, next_r, cs, cr = take(9)
    here = locate(dims)
    y, x, z, c = here
    greet(dims, here)

    def send(src, dst, ss, rs, peer):
        return pltpu.make_async_remote_copy(
            src_ref=src, dst_ref=dst, send_sem=ss, recv_sem=rs, device_id=peer, device_id_type=MESH
        )

    def halves(i, t):
        wide = wides[i]
        h = wide // 2
        a = pl.ds(pl.multiple_of(t * wide, h), h)
        b = pl.ds(pl.multiple_of(t * wide + h, h), h)
        return a, b

    def to_x(k):
        return device(dims, y, hop(x, k, X), z, c)

    def to_y(k):
        return device(dims, hop(y, k, Y), x, z, c)

    def to_z(k):
        return device(dims, y, x, hop(z, k, Z), c)

    counts = [shards[i].shape[1] // wides[i] for i in range(n)]
    bases = [sum(counts[:i]) for i in range(n)]

    def route(sends, ss, rs, i, t):
        s = lax.rem(bases[i] + t, AHEAD)
        return [
            send(src, dst, ss.at[s, n], rs.at[s, n], peer) for n, (src, dst, peer) in enumerate(sends)
        ]

    def line_copies(i, t):
        shard, whole = shards[i], wholes[i]
        columns = pl.ds(pl.multiple_of(t * wides[i], wides[i]), wides[i])
        block = (shard.at[:, columns], whole.at[y, x, z, c, :, columns])
        return route([block + (to_z(k),) for k in range(1, Z)], zs, zr, i, t)

    def own_copies(i, t):
        shard, whole = shards[i], wholes[i]
        a, b = halves(i, t)
        block_a = (shard.at[:, a], whole.at[y, x, z, c, :, a])
        block_b = (shard.at[:, b], whole.at[y, x, z, c, :, b])
        sends = [block_a + (to_x(k),) for k in range(1, X)]
        sends += [block_b + (to_y(k),) for k in range(1, Y)]
        return route(sends, zs, zr, i, t)

    def first_copies(i, t):
        whole = wholes[i]
        a, b = halves(i, t)
        block_a, block_b = whole.at[y, x, :, c, :, a], whole.at[y, x, :, c, :, b]
        sends = [(block_a, block_a, to_x(k)) for k in range(1, X)]
        sends += [(block_b, block_b, to_y(k)) for k in range(1, Y)]
        return route(sends, first_s, first_r, i, t)

    def middle_copies(i, t):
        whole = wholes[i]
        a, b = halves(i, t)
        block_a, block_b = whole.at[y, :, z, c, :, a], whole.at[:, x, z, c, :, b]
        sends = [(block_a, block_a, to_z(k)) for k in range(1, Z)]
        sends += [(block_b, block_b, to_z(k)) for k in range(1, Z)]
        return route(sends, first_s, first_r, i, t)

    def second_copies(i, t):
        whole = wholes[i]
        a, b = halves(i, t)
        block_a, block_b = whole.at[y, :, :, c, :, a], whole.at[:, x, :, c, :, b]
        sends = [(block_a, block_a, to_y(k)) for k in range(1, Y)]
        sends += [(block_b, block_b, to_x(k)) for k in range(1, X)]
        return route(sends, next_s, next_r, i, t)

    def core_copies(i, t):
        whole = wholes[i]
        wide = wides[i]
        columns = pl.ds(pl.multiple_of(t * wide, wide), wide)
        s = lax.rem(bases[i] + t, AHEAD)
        block = whole.at[:, :, :, c, :, columns]
        return [send(block, block, cs.at[s], cr.at[s], device(dims, y, x, z, 1 - c))]

    own = [
        pltpu.make_async_copy(shards[i], wholes[i].at[y, x, z, c], own_sem.at[i]) for i in range(n)
    ]
    for copy in own:
        copy.start()

    for i in range(n):
        total = counts[i]

        def either(t, inside, one, other, act):
            late = lax.rem(bases[i] + t, 3) == 2

            @pl.when(jnp.logical_and(inside, jnp.logical_not(late)))
            def _():
                for copy in one(i, t):
                    act(copy)

            @pl.when(jnp.logical_and(inside, late))
            def _():
                for copy in other(i, t):
                    act(copy)

        def start(copy):
            copy.start()

        def wait(copy):
            copy.wait()

        def step(t, _):
            either(t, t < total, line_copies, own_copies, start)

            u = t - 2
            inside = jnp.logical_and(u >= 0, u < total)
            either(u, inside, line_copies, own_copies, wait)
            either(u, inside, first_copies, middle_copies, start)

            v = t - 4
            inside = jnp.logical_and(v >= 0, v < total)
            either(v, inside, first_copies, middle_copies, wait)

            @pl.when(inside)
            def _():
                for copy in second_copies(i, v):
                    copy.start()

            w = t - 6

            @pl.when(jnp.logical_and(w >= 0, w < total))
            def _():
                for copy in second_copies(i, w):
                    copy.wait()
                for copy in core_copies(i, w):
                    copy.start()

            q = t - 8

            @pl.when(q >= 0)
            def _():
                for copy in core_copies(i, q):
                    copy.wait()

            return 0

        own[i].wait()
        lax.fori_loop(0, total + 8, step, 0)


def gather_call(dims, shards, wides, collective_id):
    Y, X, Z = dims
    n = len(shards)
    dma = lambda *shape: pltpu.SemaphoreType.DMA(shape)
    most = max(X + Y - 2, 2 * (Z - 1), 1)
    wholes = pl.pallas_call(
        functools.partial(gather_kernel, dims, wides),
        out_shape=[
            jax.ShapeDtypeStruct((Y, X, Z, 2) + shard.shape, shard.dtype) for shard in shards
        ],
        in_specs=[pl.BlockSpec(memory_space=pltpu.VMEM)] * n,
        out_specs=[pl.BlockSpec(memory_space=pl.ANY)] * n,
        scratch_shapes=[
            dma(n),
            dma(AHEAD, most), dma(AHEAD, most),
            dma(AHEAD, most), dma(AHEAD, most),
            dma(AHEAD, most), dma(AHEAD, most),
            dma(AHEAD), dma(AHEAD),
        ],
        compiler_params=pltpu.CompilerParams(
            collective_id=collective_id, has_side_effects=True
        ),
    )(*shards)
    return [whole.reshape(-1, whole.shape[-1]) for whole in wholes]


def gather_all(shard):
    return lax.all_gather(shard, ALL, axis=0, tiled=True)


def scatter_all(whole):
    return lax.psum_scatter(whole, ALL, scatter_dimension=0, tiled=True)


def shards(
    inputs,
    segment_ids,
    cotangent,
    mixer_gain,
    input_proj,
    forget_proj,
    gate_proj,
    floor_log,
    output_gain,
    output_proj,
    dense_gain,
    up_first,
    up_second,
    down_proj,
):
    width = inputs.shape[-1]
    hidden = up_first.shape[1]
    groups = inputs.shape[0] * inputs.shape[1]
    span_len = inputs.shape[2]
    rows_all = groups * span_len
    parts, place = lax.axis_size("seq"), lax.axis_index("seq")

    vectors = jnp.stack([mixer_gain, floor_log, output_gain, dense_gain], axis=1)
    vectors = jnp.pad(vectors, ((0, 0), (0, EXTRA - 4)))
    depth, deep = output_proj.shape[0], down_proj.shape[0]
    wide, narrow = 512, 256
    own_kernel = (
        depth % 16 == 0
        and deep % 16 == 0
        and parts % 2 == 0
        and width % wide == 0
        and hidden % wide == 0
    )
    dims = split_mesh(lax.axis_size("dp"), parts)
    mix_shard = jnp.concatenate([input_proj, forget_proj, gate_proj, vectors], axis=1)
    up_shard = jnp.concatenate([up_first, up_second], axis=1)
    if own_kernel:
        mix_full, out_full, up_full = gather_call(
            dims, [mix_shard, output_proj, up_shard], [256] * 3, 0
        )
    else:
        mix_full, out_full, up_full = [gather_all(a) for a in (mix_shard, output_proj, up_shard)]
    gains = mix_full[:, 3 * width : 3 * width + 4].T
    if own_kernel:
        down_proj, gains = lax.optimization_barrier((down_proj, gains))
    down_full = gather_all(down_proj)
    mixer_gain_all = gains[0:1].astype(jnp.float32)
    floor_all = gains[1:2].astype(jnp.float32)
    out_gain_all = gains[2:3].astype(jnp.float32)
    dense_gain_all = gains[3:4].astype(jnp.float32)

    seg = segment_ids.reshape(groups, span_len)
    before = lax.ppermute(seg[:, -1:], "seq", [(i, i + 1) for i in range(parts - 1)])
    before = jnp.where(place == 0, -1, before)
    link = (seg == jnp.concatenate([before, seg[:, :-1]], axis=1)).astype(jnp.float32)
    link = jnp.broadcast_to(link.reshape(rows_all, 1), (rows_all, LANES))

    flat = inputs.reshape(rows_all, width)
    scale_one = lax.rsqrt(jnp.mean(flat * flat, axis=1, keepdims=True) + norm_eps)
    scaled_one = flat * scale_one
    normed_one = (scaled_one * mixer_gain_all).astype(jnp.bfloat16)
    pre_all = dot(normed_one, mix_full)
    pre_input = pre_all[:, :width]
    pre_forget = pre_all[:, width : 2 * width]
    pre_gate = pre_all[:, 2 * width : 3 * width]

    products, partial_state = forward_scan(pre_all, floor_all, link, span_len, width)
    products = products.reshape(groups, span_len, width)
    ends = exchange(
        jnp.concatenate(
            [products[:, -1], partial_state.reshape(groups, span_len, width)[:, -1]], axis=0
        )
    )
    span_mults = ends[:, :groups]
    entering = entering_forward(span_mults, ends[:, groups:])
    states = products * entering[:, None, :] + partial_state.reshape(groups, span_len, width)
    states_flat = states.reshape(rows_all, width)
    state_scale = lax.rsqrt(jnp.mean(states_flat * states_flat, axis=1, keepdims=True) + norm_eps)
    normed_state = states_flat * state_scale
    gate_out = jax.nn.silu(pre_gate)
    mixed = (normed_state * out_gain_all * gate_out).astype(jnp.bfloat16)
    middle = flat + dot(mixed, out_full)
    scale_two = lax.rsqrt(jnp.mean(middle * middle, axis=1, keepdims=True) + norm_eps)
    scaled_two = middle * scale_two
    normed_two = (scaled_two * dense_gain_all).astype(jnp.bfloat16)
    up_both = dot(normed_two, up_full)
    up_one, up_two = up_both[:, :hidden], up_both[:, hidden:]
    activated = (jax.nn.silu(up_one) * up_two).astype(jnp.bfloat16)
    grad_flat = cotangent.reshape(rows_all, width)
    grad_dense = grad_flat.astype(jnp.bfloat16)
    down_part = contract_rows(activated, grad_dense).astype(jnp.bfloat16)
    down_full, down_part = lax.optimization_barrier((down_full, down_part))
    block_out = (middle + dot(activated, down_full)).reshape(inputs.shape)
    grad_act = contract_last(grad_dense, down_full)
    grad_up = jnp.concatenate(
        [
            (grad_act * up_two * silu_slope(up_one)).astype(jnp.bfloat16),
            (grad_act * jax.nn.silu(up_one)).astype(jnp.bfloat16),
        ],
        axis=1,
    )
    grad_normed_two = contract_last(grad_up, up_full)
    gain_two = jnp.sum(grad_normed_two * scaled_two, axis=0)
    grad_middle = grad_flat + norm_back(grad_normed_two * dense_gain_all, scaled_two, scale_two)
    grad_mixer = grad_middle.astype(jnp.bfloat16)
    grad_mix_in = contract_last(grad_mixer, out_full)
    gain_out = jnp.sum(grad_mix_in * normed_state * gate_out, axis=0)
    grad_pre_gate = (
        grad_mix_in * normed_state * out_gain_all * silu_slope(pre_gate)
    ).astype(jnp.bfloat16)
    grad_states = norm_back(grad_mix_in * out_gain_all * gate_out, normed_state, state_scale)

    local_grad, carry_mult, head_grad = backward_scan(
        grad_states, pre_all, floor_all, link, span_len, width
    )
    arriving = entering_backward(span_mults, exchange(head_grad))
    adjoint = (
        local_grad.reshape(groups, span_len, width)
        + carry_mult.reshape(groups, span_len, width) * arriving[:, None, :]
    ).reshape(rows_all, width)
    previous = jnp.concatenate([entering[:, None, :], states[:, :-1]], axis=1)
    previous = previous.reshape(rows_all, width) * link[:, :1]
    leak = jnp.exp(floor_all) * jax.nn.sigmoid(-pre_forget)
    grad_forget = adjoint * (previous - jax.nn.silu(pre_input))
    grad_pre_input = (adjoint * leak * silu_slope(pre_input)).astype(jnp.bfloat16)
    grad_pre_forget = (grad_forget * leak * jax.nn.sigmoid(pre_forget)).astype(jnp.bfloat16)
    floor_sum = -jnp.sum(grad_forget * leak, axis=0)
    grad_pre = jnp.concatenate(
        [
            grad_pre_input,
            grad_pre_forget,
            grad_pre_gate,
            jnp.zeros((rows_all, EXTRA), jnp.bfloat16),
        ],
        axis=1,
    )
    block_all = contract_last(grad_pre, mix_full)
    gain_one = jnp.sum(block_all * scaled_one, axis=0)
    input_grad = (
        grad_middle + norm_back(block_all * mixer_gain_all, scaled_one, scale_one)
    ).reshape(inputs.shape)

    low = jnp.bfloat16
    vector_sums = jnp.stack([gain_one, floor_sum, gain_out, gain_two], axis=1)
    vector_sums = jnp.pad(vector_sums, ((0, 0), (0, LANES - 4))).astype(low)
    if own_kernel:
        *grads, vector_terms = scatter_call(
            dims,
            depth,
            wide,
            [(normed_one.T, grad_pre), (mixed.T, grad_mixer), (normed_two.T, grad_up)],
            [width] * 4 + [hidden] * 2,
            vector_sums,
            1,
        )
    else:
        terms = scatter_all(
            jnp.concatenate(
                [
                    contract_rows(normed_one, grad_pre[:, : 3 * width]).astype(low),
                    contract_rows(mixed, grad_mixer).astype(low),
                    contract_rows(normed_two, grad_up).astype(low),
                    vector_sums,
                ],
                axis=1,
            )
        ).astype(jnp.float32)
        marks = [width, 2 * width, 3 * width, 4 * width]
        marks += [4 * width + hidden, 4 * width + 2 * hidden]
        *grads, vector_terms = jnp.split(terms, marks, axis=1)
    down_grad = scatter_all(down_part).astype(jnp.float32)
    return (
        block_out,
        input_grad,
        vector_terms[:, 0],
        grads[0],
        grads[1],
        grads[2],
        vector_terms[:, 1],
        vector_terms[:, 2],
        grads[3],
        vector_terms[:, 3],
        grads[4],
        grads[5],
        down_grad,
    )


def solution(mesh):
    whole = P(None, "dp", "seq", None)
    vector = P(ALL)
    matrix = P(ALL, None)
    return jax.shard_map(
        shards,
        mesh=mesh,
        in_specs=(
            whole,
            P(None, "dp", "seq"),
            whole,
            vector,
            matrix,
            matrix,
            matrix,
            vector,
            vector,
            matrix,
            vector,
            matrix,
            matrix,
            matrix,
        ),
        out_specs=(
            whole,
            whole,
            vector,
            matrix,
            matrix,
            matrix,
            vector,
            vector,
            matrix,
            vector,
            matrix,
            matrix,
            matrix,
        ),
        check_vma=False,
    )
```

```python
import functools

import jax
import jax.numpy as jnp
from jax import lax
from jax.experimental import pallas as pl
from jax.experimental.pallas import tpu as pltpu
from jax.sharding import PartitionSpec as P

norm_eps = 1e-06
ALL = ("dp", "seq")
LANES = 128
SUB = 8
MESH = pl.DeviceIdType.MESH
SLOTS = 3
AHEAD = 12
LAG = 2
EXTRA = 256


def silu_slope(values):
    logistic = jax.nn.sigmoid(values)
    return logistic * (1.0 + values * (1.0 - logistic))


def norm_back(upstream, scaled, factor):
    return factor * (upstream - scaled * jnp.mean(upstream * scaled, axis=-1, keepdims=True))


def dot(left, right):
    return jnp.dot(left, right, preferred_element_type=jnp.float32)


def contract_last(left, right):
    return lax.dot_general(
        left, right, (((1,), (1,)), ((), ())), preferred_element_type=jnp.float32
    )


def contract_rows(left, right):
    return lax.dot_general(
        left, right, (((0,), (0,)), ((), ())), preferred_element_type=jnp.float32
    )


def shift_down(values, amount, fill):
    rows = lax.broadcasted_iota(jnp.int32, values.shape, 0)
    return jnp.where(rows < amount, fill, pltpu.roll(values, amount, 0))


def shift_up(values, amount, fill):
    rows = lax.broadcasted_iota(jnp.int32, values.shape, 0)
    return jnp.where(
        rows >= SUB - amount, fill, pltpu.roll(values, SUB - amount, 0)
    )


def forward_scan_kernel(span_len, pre_input, pre_forget, floor, link, products, partial):
    tiles = span_len // SUB
    scale = jnp.exp(floor[...].astype(jnp.float32))
    width = pre_input.shape[1]
    groups = pre_input.shape[0] // span_len

    def tile(i, carries):
        out = []
        for g in range(groups):
            prod_in, state_in = carries[g]
            rows = pl.ds(pl.multiple_of(g * span_len + i * SUB, SUB), SUB)
            value = pre_input[rows, :]
            leak = scale * jax.nn.sigmoid(-pre_forget[rows, :])
            decay = (1.0 - leak) * link[rows, :1]
            state = leak * value * jax.nn.sigmoid(value)
            for step in (1, 2, 4):
                state = decay * shift_down(state, step, 0.0) + state
                decay = decay * shift_down(decay, step, 1.0)
            state = decay * state_in + state
            decay = decay * prod_in
            products[rows, :] = decay
            partial[rows, :] = state
            out.append((decay[SUB - 1 :, :], state[SUB - 1 :, :]))
        return tuple(out)

    start = (jnp.ones((1, width), jnp.float32), jnp.zeros((1, width), jnp.float32))
    lax.fori_loop(0, tiles, tile, (start,) * groups)


def backward_scan_kernel(span_len, grad_states, pre_forget, floor, link, local, carry_mult, head):
    tiles = span_len // SUB
    scale = jnp.exp(floor[...].astype(jnp.float32))
    width = grad_states.shape[1]
    groups = grad_states.shape[0] // span_len

    def tile(k, carries):
        i = tiles - 1 - k
        out = []
        for g in range(groups):
            prod_in, pass_in = carries[g]
            rows = pl.ds(pl.multiple_of(g * span_len + i * SUB, SUB), SUB)
            upstream = grad_states[rows, :]
            decay = (1.0 - scale * jax.nn.sigmoid(-pre_forget[rows, :])) * link[rows, :1]
            passed = decay * upstream
            for step in (1, 2, 4):
                passed = decay * shift_up(passed, step, 0.0) + passed
                decay = decay * shift_up(decay, step, 1.0)
            passed = decay * pass_in + passed
            decay = decay * prod_in
            local[rows, :] = upstream + shift_up(passed, 1, pass_in)
            carry_mult[rows, :] = shift_up(decay, 1, prod_in)
            out.append((decay[:1, :], passed[:1, :]))
        return tuple(out)

    start = (jnp.ones((1, width), jnp.float32), jnp.zeros((1, width), jnp.float32))
    ends = lax.fori_loop(0, tiles, tile, (start,) * groups)
    for g in range(groups):
        head[g : g + 1, :] = ends[g][1]


def scan_block(width):
    return 512 if width % 512 == 0 else width


def forward_scan(pre_all, floor, link, span_len, width):
    rows = pre_all.shape[0]
    block = scan_block(width)
    steps = width // block
    out = jax.ShapeDtypeStruct((rows, width), jnp.float32)
    return pl.pallas_call(
        lambda *refs: forward_scan_kernel(span_len, *refs),
        grid=(steps,),
        in_specs=[
            pl.BlockSpec((rows, block), lambda j: (0, j)),
            pl.BlockSpec((rows, block), lambda j: (0, j + steps)),
            pl.BlockSpec((1, block), lambda j: (0, j)),
            pl.BlockSpec((rows, LANES), lambda j: (0, 0)),
        ],
        out_specs=[pl.BlockSpec((rows, block), lambda j: (0, j))] * 2,
        out_shape=[out, out],
    )(pre_all, pre_all, floor, link)


def backward_scan(grad_states, pre_all, floor, link, span_len, width):
    rows = pre_all.shape[0]
    groups = rows // span_len
    block = scan_block(width)
    steps = width // block
    out = jax.ShapeDtypeStruct((rows, width), jnp.float32)
    return pl.pallas_call(
        lambda *refs: backward_scan_kernel(span_len, *refs),
        grid=(steps,),
        in_specs=[
            pl.BlockSpec((rows, block), lambda j: (0, j)),
            pl.BlockSpec((rows, block), lambda j: (0, j + steps)),
            pl.BlockSpec((1, block), lambda j: (0, j)),
            pl.BlockSpec((rows, LANES), lambda j: (0, 0)),
        ],
        out_specs=[pl.BlockSpec((rows, block), lambda j: (0, j))] * 2
        + [pl.BlockSpec((groups, block), lambda j: (0, j))],
        out_shape=[out, out, jax.ShapeDtypeStruct((groups, width), jnp.float32)],
    )(grad_states, pre_all, floor, link)


def exchange(value):
    return lax.all_gather(value.astype(jnp.bfloat16), "seq").astype(jnp.float32)


def entering_forward(mults, values):
    parts, place = lax.axis_size("seq"), lax.axis_index("seq")
    total = jnp.zeros_like(values[0])
    for k in range(parts - 1):
        total = jnp.where(k < place, mults[k] * total + values[k], total)
    return total


def entering_backward(mults, values):
    parts, place = lax.axis_size("seq"), lax.axis_index("seq")
    total = jnp.zeros_like(values[0])
    for k in range(parts - 1, 0, -1):
        total = jnp.where(k > place, mults[k] * total + values[k], total)
    return total


def split_mesh(dp, seq):
    side = max(d for d in range(1, dp + 1) if dp % d == 0 and d * d <= dp)
    return dp // side, side, seq // 2


def locate(dims):
    Y, X, Z = dims
    dp, seq = lax.axis_index("dp"), lax.axis_index("seq")
    return lax.div(dp, X), lax.rem(dp, X), lax.div(seq, 2), lax.rem(seq, 2)


def device(dims, y, x, z, c):
    return (y * dims[1] + x, z * 2 + c)


def hop(place, k, size):
    return lax.rem(place + k, size)


def greet(dims, here):
    Y, X, Z = dims
    y, x, z, c = here
    barrier = pltpu.get_barrier_semaphore()
    peers = [device(dims, y, x, z, 1 - c)]
    peers += [device(dims, hop(y, k, Y), x, z, c) for k in range(1, Y)]
    peers += [device(dims, y, hop(x, k, X), z, c) for k in range(1, X)]
    peers += [device(dims, y, x, hop(z, k, Z), c) for k in range(1, Z)]
    for peer in peers:
        pl.semaphore_signal(barrier, inc=1, device_id=peer, device_id_type=MESH)
    pl.semaphore_wait(barrier, len(peers))


def scatter_kernel(dims, depth, wide, pairs, spans, has_vec, *refs):
    Y, X, Z = dims
    half = wide // 2
    f32, low = jnp.float32, jnp.bfloat16
    refs = list(refs)
    take = lambda n: [refs.pop(0) for _ in range(n)]
    lefts, rights = take(pairs), take(pairs)
    vec = take(1)[0] if has_vec else None
    outs = take(len(spans))
    (part, core_in, one_a, one_b, in_a, in_b, two_a, two_b, far_a, far_b, three, line_in) = take(12)
    (mid_a, mid_b, four_a, four_b, last_a, last_b) = take(6)
    (core_s, core_r, ya_s, ya_r, xb_s, xb_r, xa_s, xa_r, yb_s, yb_r, z_s, z_r) = take(12)
    (ma_s, ma_r, mb_s, mb_r, la_s, la_r, lb_s, lb_r) = take(8)
    (core_f, ya_f, xb_f, xa_f, yb_f, z_f, ma_f, mb_f, la_f, lb_f) = take(10)
    here = locate(dims)
    y, x, z, c = here
    greet(dims, here)
    total = spans[-1][2]

    def send(src, dst, ss, rs, peer):
        return pltpu.make_async_remote_copy(
            src_ref=src, dst_ref=dst, send_sem=ss, recv_sem=rs, device_id=peer, device_id_type=MESH
        )

    late_total = total // 3
    early_total = total - late_total

    def is_late(t):
        return lax.rem(t, 3) == 2

    def late_index(t):
        return lax.div(t, 3)

    def early_index(t):
        return 2 * lax.div(t, 3) + lax.rem(t, 3)

    x_hops = [(k - 1, hop(x, k, X), hop(x, X - k, X)) for k in range(1, X)]
    y_hops = [(k - 1, hop(y, k, Y), hop(y, Y - k, Y)) for k in range(1, Y)]
    z_hops = [(k - 1, hop(z, k, Z), hop(z, Z - k, Z)) for k in range(1, Z)]
    at_x = lambda i: device(dims, y, i, z, c)
    at_y = lambda i: device(dims, i, x, z, c)
    at_z = lambda i: device(dims, y, x, i, c)

    def along(hops, at, piece, landing, ss, rs, free, s):
        return [
            (
                send(piece(to), landing.at[s, n], ss.at[s, n], rs.at[s, n], at(to)),
                free.at[n],
                at(giver),
            )
            for n, to, giver in hops
        ]

    def core_copies(t):
        s = lax.rem(t, SLOTS)
        peer = device(dims, y, x, z, 1 - c)
        copy = send(part.at[s, 1 - c], core_in.at[s], core_s.at[s], core_r.at[s], peer)
        return [(copy, core_f.at[0], peer)]

    def first_copies(t):
        s = lax.rem(t, SLOTS)
        return along(
            y_hops, at_y, lambda to: one_a.at[s, to], in_a, ya_s, ya_r, ya_f, s
        ) + along(x_hops, at_x, lambda to: one_b.at[s, to], in_b, xb_s, xb_r, xb_f, s)

    def second_copies(t):
        s, r = lax.rem(t, SLOTS), lax.rem(early_index(t), SLOTS)
        return along(
            x_hops, at_x, lambda to: two_a.at[s, to], far_a, xa_s, xa_r, xa_f, r
        ) + along(y_hops, at_y, lambda to: two_b.at[s, to], far_b, yb_s, yb_r, yb_f, r)

    def middle_copies(t):
        s, r = lax.rem(t, SLOTS), lax.rem(late_index(t), SLOTS)
        return along(
            z_hops, at_z, lambda to: two_a.at[s, :, to], mid_a, ma_s, ma_r, ma_f, r
        ) + along(z_hops, at_z, lambda to: two_b.at[s, :, to], mid_b, mb_s, mb_r, mb_f, r)

    def line_copies(t):
        s, r = lax.rem(t, SLOTS), lax.rem(early_index(t), SLOTS)
        return along(z_hops, at_z, lambda to: three.at[s, to], line_in, z_s, z_r, z_f, r)

    def last_copies(t):
        s, r = lax.rem(t, SLOTS), lax.rem(late_index(t), SLOTS)
        return along(
            x_hops, at_x, lambda to: four_a.at[s, to], last_a, la_s, la_r, la_f, r
        ) + along(y_hops, at_y, lambda to: four_b.at[s, to], last_b, lb_s, lb_r, lb_f, r)

    def begin(copies, index):
        for copy, free, _ in copies:

            @pl.when(index >= SLOTS)
            def _():
                pl.semaphore_wait(free, 1)

            copy.start()

    def arrive(copies):
        for copy, _, _ in copies:
            copy.wait()

    def release(copies, index, count):
        for _, free, giver in copies:

            @pl.when(index + SLOTS < count)
            def _():
                pl.semaphore_signal(free, inc=1, device_id=giver, device_id_type=MESH)

    def summed(own, landing, r, hops):
        value = own.astype(f32)
        for n, _, _ in hops:
            value = value + landing[r, n].astype(f32)
        return value

    def produce(t):
        s = lax.rem(t, SLOTS)
        for pair in range(pairs):
            low_t, high_t = rights_span[pair]

            @pl.when(jnp.logical_and(t >= low_t, t < high_t))
            def _():
                columns = pl.ds(pl.multiple_of((t - low_t) * wide, wide), wide)

                def block(i, _):
                    rows = Z * 2 * depth
                    first = pl.multiple_of(i * rows, rows)
                    value = jnp.dot(
                        lefts[pair][pl.ds(first, rows), :],
                        rights[pair][:, columns],
                        preferred_element_type=f32,
                    ).astype(low)
                    value = value.reshape(Z, 2, depth, wide)
                    for core in range(2):
                        part[s, core, lax.div(i, X), lax.rem(i, X)] = value[:, core]
                    return 0

                lax.fori_loop(0, Y * X, block, 0)

        if has_vec:

            @pl.when(t == total - 1)
            def _():
                def block(i, _):
                    rows = Z * 2 * depth
                    first = pl.multiple_of(i * rows, rows)
                    value = vec[pl.ds(first, rows), :].reshape(Z, 2, depth, vec.shape[1])
                    for core in range(2):
                        part[s, core, lax.div(i, X), lax.rem(i, X), :, :, : vec.shape[1]] = value[
                            :, core
                        ]
                    return 0

                lax.fori_loop(0, Y * X, block, 0)

    rights_span = []
    start = 0
    for pair in range(pairs):
        count = rights[pair].shape[1] // wide
        rights_span.append((start, start + count))
        start += count

    def step(t, _):
        @pl.when(t < total)
        def _():
            produce(t)
            begin(core_copies(t), t)

        u = t - 2

        @pl.when(jnp.logical_and(u >= 0, u < total))
        def _():
            s = lax.rem(u, SLOTS)
            copies = core_copies(u)
            arrive(copies)

            def block(i, _):
                i, j = lax.div(i, X), lax.rem(i, X)
                value = part[s, c, i, j].astype(f32) + core_in[s, i, j].astype(f32)
                value = value.astype(low)
                one_a[s, i, j] = value[:, :, :half]
                one_b[s, j, i] = value[:, :, half:]
                return 0

            lax.fori_loop(0, Y * X, block, 0)
            release(copies, u, total)
            begin(first_copies(u), u)

        v = t - 4
        inside = jnp.logical_and(v >= 0, v < total)

        @pl.when(inside)
        def _():
            s = lax.rem(v, SLOTS)
            copies = first_copies(v)
            arrive(copies)
            two_a[s] = summed(one_a[s, y], in_a, s, y_hops).astype(low)
            two_b[s] = summed(one_b[s, x], in_b, s, x_hops).astype(low)
            release(copies, v, total)

        @pl.when(jnp.logical_and(inside, jnp.logical_not(is_late(v))))
        def _():
            begin(second_copies(v), early_index(v))

        @pl.when(jnp.logical_and(inside, is_late(v)))
        def _():
            begin(middle_copies(v), late_index(v))

        w = t - 6
        inside = jnp.logical_and(w >= 0, w < total)

        @pl.when(jnp.logical_and(inside, jnp.logical_not(is_late(w))))
        def _():
            s, index = lax.rem(w, SLOTS), early_index(w)
            r = lax.rem(index, SLOTS)
            copies = second_copies(w)
            arrive(copies)
            three[s, :, :, :half] = summed(two_a[s, x], far_a, r, x_hops).astype(low)
            three[s, :, :, half:] = summed(two_b[s, y], far_b, r, y_hops).astype(low)
            release(copies, index, early_total)
            begin(line_copies(w), index)

        @pl.when(jnp.logical_and(inside, is_late(w)))
        def _():
            s, index = lax.rem(w, SLOTS), late_index(w)
            r = lax.rem(index, SLOTS)
            copies = middle_copies(w)
            arrive(copies)
            four_a[s] = summed(two_a[s, :, z], mid_a, r, z_hops).astype(low)
            four_b[s] = summed(two_b[s, :, z], mid_b, r, z_hops).astype(low)
            release(copies, index, late_total)
            begin(last_copies(w), index)

        q = t - 8

        def store(first, last, value):
            for number, (_, low_t, high_t) in enumerate(spans):

                @pl.when(jnp.logical_and(q >= low_t, q < high_t))
                def _():
                    start = pl.multiple_of((q - low_t) * wide + first, half)
                    outs[number][:, pl.ds(start, last - first)] = value

        @pl.when(jnp.logical_and(q >= 0, jnp.logical_not(is_late(q))))
        def _():
            s, index = lax.rem(q, SLOTS), early_index(q)
            r = lax.rem(index, SLOTS)
            copies = line_copies(q)
            arrive(copies)
            value = summed(three[s, z], line_in, r, z_hops)
            release(copies, index, early_total)
            store(0, wide, value)

        @pl.when(jnp.logical_and(q >= 0, is_late(q)))
        def _():
            s, index = lax.rem(q, SLOTS), late_index(q)
            r = lax.rem(index, SLOTS)
            copies = last_copies(q)
            arrive(copies)
            value_a = summed(four_a[s, x], last_a, r, x_hops)
            value_b = summed(four_b[s, y], last_b, r, y_hops)
            release(copies, index, late_total)
            store(0, half, value_a)
            store(half, wide, value_b)

        return 0

    lax.fori_loop(0, total + 8, step, 0)


def scatter_call(dims, depth, wide, pairs, widths, vec, collective_id):
    Y, X, Z = dims
    half = wide // 2
    low = jnp.bfloat16
    widths = list(widths)
    if vec is not None:
        widths.append(wide)
    spans, start = [], 0
    for n in widths:
        spans.append((n, start, start + n // wide))
        start += n // wide
    operands = [a for a, _ in pairs] + [b for _, b in pairs] + ([vec] if vec is not None else [])
    vmem = lambda *shape: pltpu.VMEM((SLOTS,) + shape, low)
    dma = lambda *shape: pltpu.SemaphoreType.DMA((SLOTS,) + shape)
    reg = lambda n: pltpu.SemaphoreType.REGULAR((n,))
    y1, x1, z1 = max(Y - 1, 1), max(X - 1, 1), max(Z - 1, 1)
    scratch = [
        vmem(2, Y, X, Z, depth, wide),
        vmem(Y, X, Z, depth, wide),
        vmem(Y, X, Z, depth, half),
        vmem(X, Y, Z, depth, half),
        vmem(y1, X, Z, depth, half),
        vmem(x1, Y, Z, depth, half),
        vmem(X, Z, depth, half),
        vmem(Y, Z, depth, half),
        vmem(x1, Z, depth, half),
        vmem(y1, Z, depth, half),
        vmem(Z, depth, wide),
        vmem(z1, depth, wide),
        vmem(z1, X, depth, half),
        vmem(z1, Y, depth, half),
        vmem(X, depth, half),
        vmem(Y, depth, half),
        vmem(x1, depth, half),
        vmem(y1, depth, half),
    ]
    scratch += [dma(), dma()]
    scratch += [dma(y1), dma(y1), dma(x1), dma(x1), dma(x1), dma(x1), dma(y1), dma(y1), dma(z1), dma(z1)]
    scratch += [dma(z1), dma(z1), dma(z1), dma(z1), dma(x1), dma(x1), dma(y1), dma(y1)]
    scratch += [reg(1), reg(y1), reg(x1), reg(x1), reg(y1), reg(z1)]
    scratch += [reg(z1), reg(z1), reg(x1), reg(y1)]
    return pl.pallas_call(
        functools.partial(
            scatter_kernel, dims, depth, wide, len(pairs), spans, vec is not None
        ),
        out_shape=[jax.ShapeDtypeStruct((depth, n), jnp.float32) for n in widths],
        in_specs=[pl.BlockSpec(memory_space=pltpu.VMEM)] * len(operands),
        out_specs=[pl.BlockSpec(memory_space=pltpu.VMEM)] * len(widths),
        scratch_shapes=scratch,
        compiler_params=pltpu.CompilerParams(
            collective_id=collective_id, has_side_effects=True, vmem_limit_bytes=60 * 2**20
        ),
    )(*operands)


def gather_kernel(dims, wides, *refs):
    Y, X, Z = dims
    refs = list(refs)
    take = lambda n: [refs.pop(0) for _ in range(n)]
    n = len(wides)
    shards, wholes = take(n), take(n)
    own_sem, zs, zr, first_s, first_r, next_s, next_r, cs, cr = take(9)
    here = locate(dims)
    y, x, z, c = here
    greet(dims, here)

    def send(src, dst, ss, rs, peer):
        return pltpu.make_async_remote_copy(
            src_ref=src, dst_ref=dst, send_sem=ss, recv_sem=rs, device_id=peer, device_id_type=MESH
        )

    def halves(i, t):
        wide = wides[i]
        h = wide // 2
        a = pl.ds(pl.multiple_of(t * wide, h), h)
        b = pl.ds(pl.multiple_of(t * wide + h, h), h)
        return a, b

    def to_x(k):
        return device(dims, y, hop(x, k, X), z, c)

    def to_y(k):
        return device(dims, hop(y, k, Y), x, z, c)

    def to_z(k):
        return device(dims, y, x, hop(z, k, Z), c)

    counts = [shards[i].shape[1] // wides[i] for i in range(n)]
    bases = [sum(counts[:i]) for i in range(n)]

    def route(sends, ss, rs, i, t):
        s = lax.rem(bases[i] + t, AHEAD)
        return [
            send(src, dst, ss.at[s, n], rs.at[s, n], peer) for n, (src, dst, peer) in enumerate(sends)
        ]

    def line_copies(i, t):
        shard, whole = shards[i], wholes[i]
        columns = pl.ds(pl.multiple_of(t * wides[i], wides[i]), wides[i])
        block = (shard.at[:, columns], whole.at[y, x, z, c, :, columns])
        return route([block + (to_z(k),) for k in range(1, Z)], zs, zr, i, t)

    def own_copies(i, t):
        shard, whole = shards[i], wholes[i]
        a, b = halves(i, t)
        block_a = (shard.at[:, a], whole.at[y, x, z, c, :, a])
        block_b = (shard.at[:, b], whole.at[y, x, z, c, :, b])
        sends = [block_a + (to_x(k),) for k in range(1, X)]
        sends += [block_b + (to_y(k),) for k in range(1, Y)]
        return route(sends, zs, zr, i, t)

    def first_copies(i, t):
        whole = wholes[i]
        a, b = halves(i, t)
        block_a, block_b = whole.at[y, x, :, c, :, a], whole.at[y, x, :, c, :, b]
        sends = [(block_a, block_a, to_x(k)) for k in range(1, X)]
        sends += [(block_b, block_b, to_y(k)) for k in range(1, Y)]
        return route(sends, first_s, first_r, i, t)

    def middle_copies(i, t):
        whole = wholes[i]
        a, b = halves(i, t)
        block_a, block_b = whole.at[y, :, z, c, :, a], whole.at[:, x, z, c, :, b]
        sends = [(block_a, block_a, to_z(k)) for k in range(1, Z)]
        sends += [(block_b, block_b, to_z(k)) for k in range(1, Z)]
        return route(sends, first_s, first_r, i, t)

    def second_copies(i, t):
        whole = wholes[i]
        a, b = halves(i, t)
        block_a, block_b = whole.at[y, :, :, c, :, a], whole.at[:, x, :, c, :, b]
        sends = [(block_a, block_a, to_y(k)) for k in range(1, Y)]
        sends += [(block_b, block_b, to_x(k)) for k in range(1, X)]
        return route(sends, next_s, next_r, i, t)

    def core_copies(i, t):
        whole = wholes[i]
        wide = wides[i]
        columns = pl.ds(pl.multiple_of(t * wide, wide), wide)
        s = lax.rem(bases[i] + t, AHEAD)
        block = whole.at[:, :, :, c, :, columns]
        return [send(block, block, cs.at[s], cr.at[s], device(dims, y, x, z, 1 - c))]

    own = [
        pltpu.make_async_copy(shards[i], wholes[i].at[y, x, z, c], own_sem.at[i]) for i in range(n)
    ]
    for copy in own:
        copy.start()
    for copy in own:
        copy.wait()
    total = sum(counts)

    def start(copy):
        copy.start()

    def wait(copy):
        copy.wait()

    def either(g, one, other, act):
        late = lax.rem(g, 3) == 2
        for i in range(n):
            inside = jnp.logical_and(g >= bases[i], g < bases[i] + counts[i])

            @pl.when(jnp.logical_and(inside, jnp.logical_not(late)))
            def _():
                for copy in one(i, g - bases[i]):
                    act(copy)

            @pl.when(jnp.logical_and(inside, late))
            def _():
                for copy in other(i, g - bases[i]):
                    act(copy)

    def every(g, one, act):
        for i in range(n):

            @pl.when(jnp.logical_and(g >= bases[i], g < bases[i] + counts[i]))
            def _():
                for copy in one(i, g - bases[i]):
                    act(copy)

    def step(g, _):
        either(g, line_copies, own_copies, start)
        either(g - LAG, line_copies, own_copies, wait)
        either(g - LAG, first_copies, middle_copies, start)
        either(g - 2 * LAG, first_copies, middle_copies, wait)
        every(g - 2 * LAG, second_copies, start)
        every(g - 3 * LAG, second_copies, wait)
        every(g - 3 * LAG, core_copies, start)
        every(g - 4 * LAG, core_copies, wait)
        return 0

    lax.fori_loop(0, total + 4 * LAG, step, 0)


def gather_call(dims, shards, wides, collective_id):
    Y, X, Z = dims
    n = len(shards)
    dma = lambda *shape: pltpu.SemaphoreType.DMA(shape)
    most = max(X + Y - 2, 2 * (Z - 1), 1)
    wholes = pl.pallas_call(
        functools.partial(gather_kernel, dims, wides),
        out_shape=[
            jax.ShapeDtypeStruct((Y, X, Z, 2) + shard.shape, shard.dtype) for shard in shards
        ],
        in_specs=[pl.BlockSpec(memory_space=pltpu.VMEM)] * n,
        out_specs=[pl.BlockSpec(memory_space=pl.ANY)] * n,
        scratch_shapes=[
            dma(n),
            dma(AHEAD, most), dma(AHEAD, most),
            dma(AHEAD, most), dma(AHEAD, most),
            dma(AHEAD, most), dma(AHEAD, most),
            dma(AHEAD), dma(AHEAD),
        ],
        compiler_params=pltpu.CompilerParams(
            collective_id=collective_id, has_side_effects=True
        ),
    )(*shards)
    return [whole.reshape(-1, whole.shape[-1]) for whole in wholes]


def gather_all(shard):
    return lax.all_gather(shard, ALL, axis=0, tiled=True)


def scatter_all(whole):
    return lax.psum_scatter(whole, ALL, scatter_dimension=0, tiled=True)


def shards(
    inputs,
    segment_ids,
    cotangent,
    mixer_gain,
    input_proj,
    forget_proj,
    gate_proj,
    floor_log,
    output_gain,
    output_proj,
    dense_gain,
    up_first,
    up_second,
    down_proj,
):
    width = inputs.shape[-1]
    hidden = up_first.shape[1]
    groups = inputs.shape[0] * inputs.shape[1]
    span_len = inputs.shape[2]
    rows_all = groups * span_len
    parts, place = lax.axis_size("seq"), lax.axis_index("seq")

    vectors = jnp.stack([mixer_gain, floor_log, output_gain, dense_gain], axis=1)
    vectors = jnp.pad(vectors, ((0, 0), (0, EXTRA - 4)))
    depth, deep = output_proj.shape[0], down_proj.shape[0]
    wide, narrow = 512, 256
    own_kernel = (
        depth % 16 == 0
        and deep % 16 == 0
        and parts % 2 == 0
        and width % wide == 0
        and hidden % wide == 0
    )
    dims = split_mesh(lax.axis_size("dp"), parts)
    mix_shard = jnp.concatenate([input_proj, forget_proj, gate_proj, vectors], axis=1)
    up_shard = jnp.concatenate([up_first, up_second], axis=1)
    if own_kernel:
        mix_full, out_full, up_full = gather_call(
            dims, [mix_shard, output_proj, up_shard], [256] * 3, 0
        )
    else:
        mix_full, out_full, up_full = [gather_all(a) for a in (mix_shard, output_proj, up_shard)]
    gains = mix_full[:, 3 * width : 3 * width + 4].T
    if own_kernel:
        down_proj, gains = lax.optimization_barrier((down_proj, gains))
    down_full = gather_all(down_proj)
    mixer_gain_all = gains[0:1].astype(jnp.float32)
    floor_all = gains[1:2].astype(jnp.float32)
    out_gain_all = gains[2:3].astype(jnp.float32)
    dense_gain_all = gains[3:4].astype(jnp.float32)

    seg = segment_ids.reshape(groups, span_len)
    before = lax.ppermute(seg[:, -1:], "seq", [(i, i + 1) for i in range(parts - 1)])
    before = jnp.where(place == 0, -1, before)
    link = (seg == jnp.concatenate([before, seg[:, :-1]], axis=1)).astype(jnp.float32)
    link = jnp.broadcast_to(link.reshape(rows_all, 1), (rows_all, LANES))

    flat = inputs.reshape(rows_all, width)
    scale_one = lax.rsqrt(jnp.mean(flat * flat, axis=1, keepdims=True) + norm_eps)
    scaled_one = flat * scale_one
    normed_one = (scaled_one * mixer_gain_all).astype(jnp.bfloat16)
    pre_all = dot(normed_one, mix_full)
    pre_input = pre_all[:, :width]
    pre_forget = pre_all[:, width : 2 * width]
    pre_gate = pre_all[:, 2 * width : 3 * width]

    products, partial_state = forward_scan(pre_all, floor_all, link, span_len, width)
    products = products.reshape(groups, span_len, width)
    ends = exchange(
        jnp.concatenate(
            [products[:, -1], partial_state.reshape(groups, span_len, width)[:, -1]], axis=0
        )
    )
    span_mults = ends[:, :groups]
    entering = entering_forward(span_mults, ends[:, groups:])
    states = products * entering[:, None, :] + partial_state.reshape(groups, span_len, width)
    states_flat = states.reshape(rows_all, width)
    state_scale = lax.rsqrt(jnp.mean(states_flat * states_flat, axis=1, keepdims=True) + norm_eps)
    normed_state = states_flat * state_scale
    gate_out = jax.nn.silu(pre_gate)
    mixed = (normed_state * out_gain_all * gate_out).astype(jnp.bfloat16)
    middle = flat + dot(mixed, out_full)
    scale_two = lax.rsqrt(jnp.mean(middle * middle, axis=1, keepdims=True) + norm_eps)
    scaled_two = middle * scale_two
    normed_two = (scaled_two * dense_gain_all).astype(jnp.bfloat16)
    up_both = dot(normed_two, up_full)
    up_one, up_two = up_both[:, :hidden], up_both[:, hidden:]
    activated = (jax.nn.silu(up_one) * up_two).astype(jnp.bfloat16)
    grad_flat = cotangent.reshape(rows_all, width)
    grad_dense = grad_flat.astype(jnp.bfloat16)
    down_part = contract_rows(activated, grad_dense).astype(jnp.bfloat16)
    down_full, down_part = lax.optimization_barrier((down_full, down_part))
    block_out = (middle + dot(activated, down_full)).reshape(inputs.shape)
    grad_act = contract_last(grad_dense, down_full)
    grad_up = jnp.concatenate(
        [
            (grad_act * up_two * silu_slope(up_one)).astype(jnp.bfloat16),
            (grad_act * jax.nn.silu(up_one)).astype(jnp.bfloat16),
        ],
        axis=1,
    )
    grad_normed_two = contract_last(grad_up, up_full)
    gain_two = jnp.sum(grad_normed_two * scaled_two, axis=0)
    grad_middle = grad_flat + norm_back(grad_normed_two * dense_gain_all, scaled_two, scale_two)
    grad_mixer = grad_middle.astype(jnp.bfloat16)
    grad_mix_in = contract_last(grad_mixer, out_full)
    gain_out = jnp.sum(grad_mix_in * normed_state * gate_out, axis=0)
    grad_pre_gate = (
        grad_mix_in * normed_state * out_gain_all * silu_slope(pre_gate)
    ).astype(jnp.bfloat16)
    grad_states = norm_back(grad_mix_in * out_gain_all * gate_out, normed_state, state_scale)

    local_grad, carry_mult, head_grad = backward_scan(
        grad_states, pre_all, floor_all, link, span_len, width
    )
    arriving = entering_backward(span_mults, exchange(head_grad))
    adjoint = (
        local_grad.reshape(groups, span_len, width)
        + carry_mult.reshape(groups, span_len, width) * arriving[:, None, :]
    ).reshape(rows_all, width)
    previous = jnp.concatenate([entering[:, None, :], states[:, :-1]], axis=1)
    previous = previous.reshape(rows_all, width) * link[:, :1]
    leak = jnp.exp(floor_all) * jax.nn.sigmoid(-pre_forget)
    grad_forget = adjoint * (previous - jax.nn.silu(pre_input))
    grad_pre_input = (adjoint * leak * silu_slope(pre_input)).astype(jnp.bfloat16)
    grad_pre_forget = (grad_forget * leak * jax.nn.sigmoid(pre_forget)).astype(jnp.bfloat16)
    floor_sum = -jnp.sum(grad_forget * leak, axis=0)
    grad_pre = jnp.concatenate(
        [
            grad_pre_input,
            grad_pre_forget,
            grad_pre_gate,
            jnp.zeros((rows_all, EXTRA), jnp.bfloat16),
        ],
        axis=1,
    )
    block_all = contract_last(grad_pre, mix_full)
    gain_one = jnp.sum(block_all * scaled_one, axis=0)
    input_grad = (
        grad_middle + norm_back(block_all * mixer_gain_all, scaled_one, scale_one)
    ).reshape(inputs.shape)

    low = jnp.bfloat16
    vector_sums = jnp.stack([gain_one, floor_sum, gain_out, gain_two], axis=1)
    vector_sums = jnp.pad(vector_sums, ((0, 0), (0, LANES - 4))).astype(low)
    if own_kernel:
        *grads, vector_terms = scatter_call(
            dims,
            depth,
            wide,
            [(normed_one.T, grad_pre), (mixed.T, grad_mixer), (normed_two.T, grad_up)],
            [width] * 4 + [hidden] * 2,
            vector_sums,
            1,
        )
    else:
        terms = scatter_all(
            jnp.concatenate(
                [
                    contract_rows(normed_one, grad_pre[:, : 3 * width]).astype(low),
                    contract_rows(mixed, grad_mixer).astype(low),
                    contract_rows(normed_two, grad_up).astype(low),
                    vector_sums,
                ],
                axis=1,
            )
        ).astype(jnp.float32)
        marks = [width, 2 * width, 3 * width, 4 * width]
        marks += [4 * width + hidden, 4 * width + 2 * hidden]
        *grads, vector_terms = jnp.split(terms, marks, axis=1)
    down_grad = scatter_all(down_part).astype(jnp.float32)
    return (
        block_out,
        input_grad,
        vector_terms[:, 0],
        grads[0],
        grads[1],
        grads[2],
        vector_terms[:, 1],
        vector_terms[:, 2],
        grads[3],
        vector_terms[:, 3],
        grads[4],
        grads[5],
        down_grad,
    )


def solution(mesh):
    whole = P(None, "dp", "seq", None)
    vector = P(ALL)
    matrix = P(ALL, None)
    return jax.shard_map(
        shards,
        mesh=mesh,
        in_specs=(
            whole,
            P(None, "dp", "seq"),
            whole,
            vector,
            matrix,
            matrix,
            matrix,
            vector,
            vector,
            matrix,
            vector,
            matrix,
            matrix,
            matrix,
        ),
        out_specs=(
            whole,
            whole,
            vector,
            matrix,
            matrix,
            matrix,
            vector,
            vector,
            matrix,
            vector,
            matrix,
            matrix,
            matrix,
        ),
        check_vma=False,
    )
```

```python
import functools

import jax
import jax.numpy as jnp
from jax import lax
from jax.experimental import pallas as pl
from jax.experimental.pallas import tpu as pltpu
from jax.sharding import PartitionSpec as P

norm_eps = 1e-06
ALL = ("dp", "seq")
LANES = 128
SUB = 8
MESH = pl.DeviceIdType.MESH
SLOTS = 3
AHEAD = 12
LAG = 2
EXTRA = 256


def silu_slope(values):
    logistic = jax.nn.sigmoid(values)
    return logistic * (1.0 + values * (1.0 - logistic))


def norm_back(upstream, scaled, factor):
    return factor * (upstream - scaled * jnp.mean(upstream * scaled, axis=-1, keepdims=True))


def dot(left, right):
    return jnp.dot(left, right, preferred_element_type=jnp.float32)


def contract_last(left, right):
    return lax.dot_general(
        left, right, (((1,), (1,)), ((), ())), preferred_element_type=jnp.float32
    )


def contract_rows(left, right):
    return lax.dot_general(
        left, right, (((0,), (0,)), ((), ())), preferred_element_type=jnp.float32
    )


def shift_down(values, amount, fill):
    rows = lax.broadcasted_iota(jnp.int32, values.shape, 0)
    return jnp.where(rows < amount, fill, pltpu.roll(values, amount, 0))


def shift_up(values, amount, fill):
    rows = lax.broadcasted_iota(jnp.int32, values.shape, 0)
    return jnp.where(
        rows >= SUB - amount, fill, pltpu.roll(values, SUB - amount, 0)
    )


def forward_scan_kernel(span_len, pre_input, pre_forget, floor, link, products, partial):
    tiles = span_len // SUB
    scale = jnp.exp(floor[...].astype(jnp.float32))
    width = pre_input.shape[1]
    groups = pre_input.shape[0] // span_len

    def tile(i, carries):
        out = []
        for g in range(groups):
            prod_in, state_in = carries[g]
            rows = pl.ds(pl.multiple_of(g * span_len + i * SUB, SUB), SUB)
            value = pre_input[rows, :]
            leak = scale * jax.nn.sigmoid(-pre_forget[rows, :])
            decay = (1.0 - leak) * link[rows, :1]
            state = leak * value * jax.nn.sigmoid(value)
            for step in (1, 2, 4):
                state = decay * shift_down(state, step, 0.0) + state
                decay = decay * shift_down(decay, step, 1.0)
            state = decay * state_in + state
            decay = decay * prod_in
            products[rows, :] = decay
            partial[rows, :] = state
            out.append((decay[SUB - 1 :, :], state[SUB - 1 :, :]))
        return tuple(out)

    start = (jnp.ones((1, width), jnp.float32), jnp.zeros((1, width), jnp.float32))
    lax.fori_loop(0, tiles, tile, (start,) * groups)


def backward_scan_kernel(span_len, grad_states, pre_forget, floor, link, local, carry_mult, head):
    tiles = span_len // SUB
    scale = jnp.exp(floor[...].astype(jnp.float32))
    width = grad_states.shape[1]
    groups = grad_states.shape[0] // span_len

    def tile(k, carries):
        i = tiles - 1 - k
        out = []
        for g in range(groups):
            prod_in, pass_in = carries[g]
            rows = pl.ds(pl.multiple_of(g * span_len + i * SUB, SUB), SUB)
            upstream = grad_states[rows, :]
            decay = (1.0 - scale * jax.nn.sigmoid(-pre_forget[rows, :])) * link[rows, :1]
            passed = decay * upstream
            for step in (1, 2, 4):
                passed = decay * shift_up(passed, step, 0.0) + passed
                decay = decay * shift_up(decay, step, 1.0)
            passed = decay * pass_in + passed
            decay = decay * prod_in
            local[rows, :] = upstream + shift_up(passed, 1, pass_in)
            carry_mult[rows, :] = shift_up(decay, 1, prod_in)
            out.append((decay[:1, :], passed[:1, :]))
        return tuple(out)

    start = (jnp.ones((1, width), jnp.float32), jnp.zeros((1, width), jnp.float32))
    ends = lax.fori_loop(0, tiles, tile, (start,) * groups)
    for g in range(groups):
        head[g : g + 1, :] = ends[g][1]


def scan_block(width):
    return 512 if width % 512 == 0 else width


def forward_scan(pre_all, floor, link, span_len, width):
    rows = pre_all.shape[0]
    block = scan_block(width)
    steps = width // block
    out = jax.ShapeDtypeStruct((rows, width), jnp.float32)
    return pl.pallas_call(
        lambda *refs: forward_scan_kernel(span_len, *refs),
        grid=(steps,),
        in_specs=[
            pl.BlockSpec((rows, block), lambda j: (0, j)),
            pl.BlockSpec((rows, block), lambda j: (0, j + steps)),
            pl.BlockSpec((1, block), lambda j: (0, j)),
            pl.BlockSpec((rows, LANES), lambda j: (0, 0)),
        ],
        out_specs=[pl.BlockSpec((rows, block), lambda j: (0, j))] * 2,
        out_shape=[out, out],
    )(pre_all, pre_all, floor, link)


def backward_scan(grad_states, pre_all, floor, link, span_len, width):
    rows = pre_all.shape[0]
    groups = rows // span_len
    block = scan_block(width)
    steps = width // block
    out = jax.ShapeDtypeStruct((rows, width), jnp.float32)
    return pl.pallas_call(
        lambda *refs: backward_scan_kernel(span_len, *refs),
        grid=(steps,),
        in_specs=[
            pl.BlockSpec((rows, block), lambda j: (0, j)),
            pl.BlockSpec((rows, block), lambda j: (0, j + steps)),
            pl.BlockSpec((1, block), lambda j: (0, j)),
            pl.BlockSpec((rows, LANES), lambda j: (0, 0)),
        ],
        out_specs=[pl.BlockSpec((rows, block), lambda j: (0, j))] * 2
        + [pl.BlockSpec((groups, block), lambda j: (0, j))],
        out_shape=[out, out, jax.ShapeDtypeStruct((groups, width), jnp.float32)],
    )(grad_states, pre_all, floor, link)


def exchange(value):
    return lax.all_gather(value.astype(jnp.bfloat16), "seq").astype(jnp.float32)


def entering_forward(mults, values):
    parts, place = lax.axis_size("seq"), lax.axis_index("seq")
    total = jnp.zeros_like(values[0])
    for k in range(parts - 1):
        total = jnp.where(k < place, mults[k] * total + values[k], total)
    return total


def entering_backward(mults, values):
    parts, place = lax.axis_size("seq"), lax.axis_index("seq")
    total = jnp.zeros_like(values[0])
    for k in range(parts - 1, 0, -1):
        total = jnp.where(k > place, mults[k] * total + values[k], total)
    return total


def split_mesh(dp, seq):
    side = max(d for d in range(1, dp + 1) if dp % d == 0 and d * d <= dp)
    return dp // side, side, seq // 2


def locate(dims):
    Y, X, Z = dims
    dp, seq = lax.axis_index("dp"), lax.axis_index("seq")
    return lax.div(dp, X), lax.rem(dp, X), lax.div(seq, 2), lax.rem(seq, 2)


def device(dims, y, x, z, c):
    return (y * dims[1] + x, z * 2 + c)


def hop(place, k, size):
    return lax.rem(place + k, size)


def greet(dims, here):
    Y, X, Z = dims
    y, x, z, c = here
    barrier = pltpu.get_barrier_semaphore()
    peers = [device(dims, y, x, z, 1 - c)]
    peers += [device(dims, hop(y, k, Y), x, z, c) for k in range(1, Y)]
    peers += [device(dims, y, hop(x, k, X), z, c) for k in range(1, X)]
    peers += [device(dims, y, x, hop(z, k, Z), c) for k in range(1, Z)]
    for peer in peers:
        pl.semaphore_signal(barrier, inc=1, device_id=peer, device_id_type=MESH)
    pl.semaphore_wait(barrier, len(peers))


def scatter_kernel(dims, depth, wide, sides, spans, *refs):
    Y, X, Z = dims
    half = wide // 2
    f32, low = jnp.float32, jnp.bfloat16
    refs = list(refs)
    take = lambda n: [refs.pop(0) for _ in range(n)]
    pairs, left_count = len(sides), max(sides) + 1
    far_lefts, far_rights = take(left_count), take(pairs)
    far_act, job_weight, far_base, vec = take(4)
    outs = take(len(spans))
    (job_out,) = take(1)
    lefts, rights = take(left_count), take(pairs)
    act, slab, load_sem, slab_sem = take(4)
    (part, core_in, one_a, one_b, in_a, in_b, two_a, two_b, far_a, far_b, three, line_in) = take(12)
    (mid_a, mid_b, four_a, four_b, last_a, last_b) = take(6)
    (core_s, core_r, ya_s, ya_r, xb_s, xb_r, xa_s, xa_r, yb_s, yb_r, z_s, z_r) = take(12)
    (ma_s, ma_r, mb_s, mb_r, la_s, la_r, lb_s, lb_r) = take(8)
    (core_f, ya_f, xb_f, xa_f, yb_f, z_f, ma_f, mb_f, la_f, lb_f) = take(10)
    sources = [far_lefts[0], far_rights[0], far_act, far_base] + far_lefts[1:] + far_rights[1:]
    targets = [lefts[0], rights[0], act, job_out] + lefts[1:] + rights[1:]
    loads = [
        pltpu.make_async_copy(source, target, load_sem.at[n])
        for n, (source, target) in enumerate(zip(sources, targets))
    ]
    for load in loads:
        load.start()
    here = locate(dims)
    y, x, z, c = here
    greet(dims, here)
    total = spans[-1][2]
    left_loads = [loads[0]] + loads[4 : 3 + left_count]
    right_loads = [loads[1]] + loads[3 + left_count :]
    slab_rows = slab.shape[1]
    slabs = job_weight.shape[0] // slab_rows

    def fetch(k):
        rows = pl.ds(pl.multiple_of(k * slab_rows, slab_rows), slab_rows)
        s = lax.rem(k, 2)
        return pltpu.make_async_copy(job_weight.at[rows], slab.at[s], slab_sem.at[s])

    def job(k):
        @pl.when(k == -1)
        def _():
            fetch(0).start()

        @pl.when(k == 0)
        def _():
            loads[2].wait()
            loads[3].wait()

        @pl.when(jnp.logical_and(k >= 0, k < slabs))
        def _():
            @pl.when(k + 1 < slabs)
            def _():
                fetch(k + 1).start()

            fetch(k).wait()
            s = lax.rem(k, 2)
            depths = pl.ds(pl.multiple_of(k * slab_rows, slab_rows), slab_rows)
            for first in range(0, job_out.shape[1], wide):
                job_out[:, first : first + wide] += jnp.dot(
                    act[:, depths],
                    slab[s, :, first : first + wide],
                    preferred_element_type=f32,
                )

    def send(src, dst, ss, rs, peer):
        return pltpu.make_async_remote_copy(
            src_ref=src, dst_ref=dst, send_sem=ss, recv_sem=rs, device_id=peer, device_id_type=MESH
        )

    late_total = total // 3
    early_total = total - late_total

    def is_late(t):
        return lax.rem(t, 3) == 2

    def late_index(t):
        return lax.div(t, 3)

    def early_index(t):
        return 2 * lax.div(t, 3) + lax.rem(t, 3)

    x_hops = [(k - 1, hop(x, k, X), hop(x, X - k, X)) for k in range(1, X)]
    y_hops = [(k - 1, hop(y, k, Y), hop(y, Y - k, Y)) for k in range(1, Y)]
    z_hops = [(k - 1, hop(z, k, Z), hop(z, Z - k, Z)) for k in range(1, Z)]
    at_x = lambda i: device(dims, y, i, z, c)
    at_y = lambda i: device(dims, i, x, z, c)
    at_z = lambda i: device(dims, y, x, i, c)

    def along(hops, at, piece, landing, ss, rs, free, s):
        return [
            (
                send(piece(to), landing.at[s, n], ss.at[s, n], rs.at[s, n], at(to)),
                free.at[n],
                at(giver),
            )
            for n, to, giver in hops
        ]

    def core_copies(t):
        s = lax.rem(t, SLOTS)
        peer = device(dims, y, x, z, 1 - c)
        copy = send(part.at[s, 1 - c], core_in.at[s], core_s.at[s], core_r.at[s], peer)
        return [(copy, core_f.at[0], peer)]

    def first_copies(t):
        s = lax.rem(t, SLOTS)
        return along(
            y_hops, at_y, lambda to: one_a.at[s, to], in_a, ya_s, ya_r, ya_f, s
        ) + along(x_hops, at_x, lambda to: one_b.at[s, to], in_b, xb_s, xb_r, xb_f, s)

    def second_copies(t):
        s, r = lax.rem(t, SLOTS), lax.rem(early_index(t), SLOTS)
        return along(
            x_hops, at_x, lambda to: two_a.at[s, to], far_a, xa_s, xa_r, xa_f, r
        ) + along(y_hops, at_y, lambda to: two_b.at[s, to], far_b, yb_s, yb_r, yb_f, r)

    def middle_copies(t):
        s, r = lax.rem(t, SLOTS), lax.rem(late_index(t), SLOTS)
        return along(
            z_hops, at_z, lambda to: two_a.at[s, :, to], mid_a, ma_s, ma_r, ma_f, r
        ) + along(z_hops, at_z, lambda to: two_b.at[s, :, to], mid_b, mb_s, mb_r, mb_f, r)

    def line_copies(t):
        s, r = lax.rem(t, SLOTS), lax.rem(early_index(t), SLOTS)
        return along(z_hops, at_z, lambda to: three.at[s, to], line_in, z_s, z_r, z_f, r)

    def last_copies(t):
        s, r = lax.rem(t, SLOTS), lax.rem(late_index(t), SLOTS)
        return along(
            x_hops, at_x, lambda to: four_a.at[s, to], last_a, la_s, la_r, la_f, r
        ) + along(y_hops, at_y, lambda to: four_b.at[s, to], last_b, lb_s, lb_r, lb_f, r)

    def begin(copies, index):
        for copy, free, _ in copies:

            @pl.when(index >= SLOTS)
            def _():
                pl.semaphore_wait(free, 1)

            copy.start()

    def arrive(copies):
        for copy, _, _ in copies:
            copy.wait()

    def release(copies, index, count):
        for _, free, giver in copies:

            @pl.when(index + SLOTS < count)
            def _():
                pl.semaphore_signal(free, inc=1, device_id=giver, device_id_type=MESH)

    def summed(own, landing, r, hops):
        value = own.astype(f32)
        for n, _, _ in hops:
            value = value + landing[r, n].astype(f32)
        return value

    def produce(t):
        s = lax.rem(t, SLOTS)
        for pair in range(pairs):
            low_t, high_t = rights_span[pair]
            left = lefts[sides[pair]]

            @pl.when(t == low_t)
            def _():
                right_loads[pair].wait()
                if sides.index(sides[pair]) == pair:
                    left_loads[sides[pair]].wait()

            @pl.when(jnp.logical_and(t >= low_t, t < high_t))
            def _():
                columns = pl.ds(pl.multiple_of((t - low_t) * wide, wide), wide)

                def block(i, _):
                    rows = Z * 2 * depth
                    first = pl.multiple_of(i * rows, rows)
                    value = jnp.dot(
                        left[pl.ds(first, rows), :],
                        rights[pair][:, columns],
                        preferred_element_type=f32,
                    ).astype(low)
                    value = value.reshape(Z, 2, depth, wide)
                    for core in range(2):
                        part[s, core, lax.div(i, X), lax.rem(i, X)] = value[:, core]
                    return 0

                lax.fori_loop(0, Y * X, block, 0)

        @pl.when(t == total - 1)
        def _():
            def block(i, _):
                rows = Z * 2 * depth
                first = pl.multiple_of(i * rows, rows)
                value = vec[pl.ds(first, rows), :].reshape(Z, 2, depth, vec.shape[1])
                for core in range(2):
                    part[s, core, lax.div(i, X), lax.rem(i, X), :, :, : vec.shape[1]] = value[
                        :, core
                    ]
                return 0

            lax.fori_loop(0, Y * X, block, 0)

    rights_span = []
    start = 0
    for pair in range(pairs):
        count = rights[pair].shape[1] // wide
        rights_span.append((start, start + count))
        start += count

    def step(t, _):
        @pl.when(t < total)
        def _():
            produce(t)
            begin(core_copies(t), t)

        job(t - 2)

        u = t - 2

        @pl.when(jnp.logical_and(u >= 0, u < total))
        def _():
            s = lax.rem(u, SLOTS)
            copies = core_copies(u)
            arrive(copies)

            def block(i, _):
                i, j = lax.div(i, X), lax.rem(i, X)
                value = part[s, c, i, j].astype(f32) + core_in[s, i, j].astype(f32)
                value = value.astype(low)
                one_a[s, i, j] = value[:, :, :half]
                one_b[s, j, i] = value[:, :, half:]
                return 0

            lax.fori_loop(0, Y * X, block, 0)
            release(copies, u, total)
            begin(first_copies(u), u)

        v = t - 4
        inside = jnp.logical_and(v >= 0, v < total)

        @pl.when(inside)
        def _():
            s = lax.rem(v, SLOTS)
            copies = first_copies(v)
            arrive(copies)
            two_a[s] = summed(one_a[s, y], in_a, s, y_hops).astype(low)
            two_b[s] = summed(one_b[s, x], in_b, s, x_hops).astype(low)
            release(copies, v, total)

        @pl.when(jnp.logical_and(inside, jnp.logical_not(is_late(v))))
        def _():
            begin(second_copies(v), early_index(v))

        @pl.when(jnp.logical_and(inside, is_late(v)))
        def _():
            begin(middle_copies(v), late_index(v))

        w = t - 6
        inside = jnp.logical_and(w >= 0, w < total)

        @pl.when(jnp.logical_and(inside, jnp.logical_not(is_late(w))))
        def _():
            s, index = lax.rem(w, SLOTS), early_index(w)
            r = lax.rem(index, SLOTS)
            copies = second_copies(w)
            arrive(copies)
            three[s, :, :, :half] = summed(two_a[s, x], far_a, r, x_hops).astype(low)
            three[s, :, :, half:] = summed(two_b[s, y], far_b, r, y_hops).astype(low)
            release(copies, index, early_total)
            begin(line_copies(w), index)

        @pl.when(jnp.logical_and(inside, is_late(w)))
        def _():
            s, index = lax.rem(w, SLOTS), late_index(w)
            r = lax.rem(index, SLOTS)
            copies = middle_copies(w)
            arrive(copies)
            four_a[s] = summed(two_a[s, :, z], mid_a, r, z_hops).astype(low)
            four_b[s] = summed(two_b[s, :, z], mid_b, r, z_hops).astype(low)
            release(copies, index, late_total)
            begin(last_copies(w), index)

        q = t - 8

        def store(first, last, value):
            for number, (_, low_t, high_t) in enumerate(spans):

                @pl.when(jnp.logical_and(q >= low_t, q < high_t))
                def _():
                    start = pl.multiple_of((q - low_t) * wide + first, half)
                    outs[number][:, pl.ds(start, last - first)] = value

        @pl.when(jnp.logical_and(q >= 0, jnp.logical_not(is_late(q))))
        def _():
            s, index = lax.rem(q, SLOTS), early_index(q)
            r = lax.rem(index, SLOTS)
            copies = line_copies(q)
            arrive(copies)
            value = summed(three[s, z], line_in, r, z_hops)
            release(copies, index, early_total)
            store(0, wide, value)

        @pl.when(jnp.logical_and(q >= 0, is_late(q)))
        def _():
            s, index = lax.rem(q, SLOTS), late_index(q)
            r = lax.rem(index, SLOTS)
            copies = last_copies(q)
            arrive(copies)
            value_a = summed(four_a[s, x], last_a, r, x_hops)
            value_b = summed(four_b[s, y], last_b, r, y_hops)
            release(copies, index, late_total)
            store(0, half, value_a)
            store(half, wide, value_b)

        return 0

    lax.fori_loop(0, total + 8, step, 0)


def scatter_call(dims, depth, wide, lefts, sides, rights, widths, vec, job, collective_id):
    Y, X, Z = dims
    half = wide // 2
    low = jnp.bfloat16
    widths = list(widths) + [wide]
    spans, start = [], 0
    for n in widths:
        spans.append((n, start, start + n // wide))
        start += n // wide
    act, weight, base = job
    slab_rows = wide
    assert weight.shape[0] % slab_rows == 0 and weight.shape[0] // slab_rows + 2 < start
    operands = list(lefts) + list(rights) + [act, weight, base, vec]
    vmem = lambda *shape: pltpu.VMEM((SLOTS,) + shape, low)
    dma = lambda *shape: pltpu.SemaphoreType.DMA((SLOTS,) + shape)
    reg = lambda n: pltpu.SemaphoreType.REGULAR((n,))
    y1, x1, z1 = max(Y - 1, 1), max(X - 1, 1), max(Z - 1, 1)
    scratch = [pltpu.VMEM(a.shape, a.dtype) for a in list(lefts) + list(rights) + [act]]
    scratch += [
        pltpu.VMEM((2, slab_rows, weight.shape[1]), weight.dtype),
        pltpu.SemaphoreType.DMA((len(operands) - 2,)),
        pltpu.SemaphoreType.DMA((2,)),
    ]
    scratch += [
        vmem(2, Y, X, Z, depth, wide),
        vmem(Y, X, Z, depth, wide),
        vmem(Y, X, Z, depth, half),
        vmem(X, Y, Z, depth, half),
        vmem(y1, X, Z, depth, half),
        vmem(x1, Y, Z, depth, half),
        vmem(X, Z, depth, half),
        vmem(Y, Z, depth, half),
        vmem(x1, Z, depth, half),
        vmem(y1, Z, depth, half),
        vmem(Z, depth, wide),
        vmem(z1, depth, wide),
        vmem(z1, X, depth, half),
        vmem(z1, Y, depth, half),
        vmem(X, depth, half),
        vmem(Y, depth, half),
        vmem(x1, depth, half),
        vmem(y1, depth, half),
    ]
    scratch += [dma(), dma()]
    scratch += [dma(y1), dma(y1), dma(x1), dma(x1), dma(x1), dma(x1), dma(y1), dma(y1), dma(z1), dma(z1)]
    scratch += [dma(z1), dma(z1), dma(z1), dma(z1), dma(x1), dma(x1), dma(y1), dma(y1)]
    scratch += [reg(1), reg(y1), reg(x1), reg(x1), reg(y1), reg(z1)]
    scratch += [reg(z1), reg(z1), reg(x1), reg(y1)]
    return pl.pallas_call(
        functools.partial(scatter_kernel, dims, depth, wide, tuple(sides), spans),
        out_shape=[jax.ShapeDtypeStruct((depth, n), jnp.float32) for n in widths]
        + [jax.ShapeDtypeStruct(base.shape, base.dtype)],
        in_specs=[pl.BlockSpec(memory_space=pl.ANY)] * (len(operands) - 1)
        + [pl.BlockSpec(memory_space=pltpu.VMEM)],
        out_specs=[pl.BlockSpec(memory_space=pltpu.VMEM)] * (len(widths) + 1),
        scratch_shapes=scratch,
        compiler_params=pltpu.CompilerParams(
            collective_id=collective_id, has_side_effects=True, vmem_limit_bytes=60 * 2**20
        ),
    )(*operands)


def gather_kernel(dims, wides, *refs):
    Y, X, Z = dims
    refs = list(refs)
    take = lambda n: [refs.pop(0) for _ in range(n)]
    n = len(wides)
    shards, wholes = take(n), take(n)
    own_sem, zs, zr, first_s, first_r, next_s, next_r, cs, cr = take(9)
    here = locate(dims)
    y, x, z, c = here
    greet(dims, here)

    def send(src, dst, ss, rs, peer):
        return pltpu.make_async_remote_copy(
            src_ref=src, dst_ref=dst, send_sem=ss, recv_sem=rs, device_id=peer, device_id_type=MESH
        )

    def halves(i, t):
        wide = wides[i]
        h = wide // 2
        a = pl.ds(pl.multiple_of(t * wide, h), h)
        b = pl.ds(pl.multiple_of(t * wide + h, h), h)
        return a, b

    def to_x(k):
        return device(dims, y, hop(x, k, X), z, c)

    def to_y(k):
        return device(dims, hop(y, k, Y), x, z, c)

    def to_z(k):
        return device(dims, y, x, hop(z, k, Z), c)

    counts = [shards[i].shape[1] // wides[i] for i in range(n)]
    bases = [sum(counts[:i]) for i in range(n)]

    def route(sends, ss, rs, i, t):
        s = lax.rem(bases[i] + t, AHEAD)
        return [
            send(src, dst, ss.at[s, n], rs.at[s, n], peer) for n, (src, dst, peer) in enumerate(sends)
        ]

    def line_copies(i, t):
        shard, whole = shards[i], wholes[i]
        columns = pl.ds(pl.multiple_of(t * wides[i], wides[i]), wides[i])
        block = (shard.at[:, columns], whole.at[y, x, z, c, :, columns])
        return route([block + (to_z(k),) for k in range(1, Z)], zs, zr, i, t)

    def own_copies(i, t):
        shard, whole = shards[i], wholes[i]
        a, b = halves(i, t)
        block_a = (shard.at[:, a], whole.at[y, x, z, c, :, a])
        block_b = (shard.at[:, b], whole.at[y, x, z, c, :, b])
        sends = [block_a + (to_x(k),) for k in range(1, X)]
        sends += [block_b + (to_y(k),) for k in range(1, Y)]
        return route(sends, zs, zr, i, t)

    def first_copies(i, t):
        whole = wholes[i]
        a, b = halves(i, t)
        block_a, block_b = whole.at[y, x, :, c, :, a], whole.at[y, x, :, c, :, b]
        sends = [(block_a, block_a, to_x(k)) for k in range(1, X)]
        sends += [(block_b, block_b, to_y(k)) for k in range(1, Y)]
        return route(sends, first_s, first_r, i, t)

    def middle_copies(i, t):
        whole = wholes[i]
        a, b = halves(i, t)
        block_a, block_b = whole.at[y, :, z, c, :, a], whole.at[:, x, z, c, :, b]
        sends = [(block_a, block_a, to_z(k)) for k in range(1, Z)]
        sends += [(block_b, block_b, to_z(k)) for k in range(1, Z)]
        return route(sends, first_s, first_r, i, t)

    def second_copies(i, t):
        whole = wholes[i]
        a, b = halves(i, t)
        block_a, block_b = whole.at[y, :, :, c, :, a], whole.at[:, x, :, c, :, b]
        sends = [(block_a, block_a, to_y(k)) for k in range(1, Y)]
        sends += [(block_b, block_b, to_x(k)) for k in range(1, X)]
        return route(sends, next_s, next_r, i, t)

    def core_copies(i, t):
        whole = wholes[i]
        wide = wides[i]
        columns = pl.ds(pl.multiple_of(t * wide, wide), wide)
        s = lax.rem(bases[i] + t, AHEAD)
        block = whole.at[:, :, :, c, :, columns]
        return [send(block, block, cs.at[s], cr.at[s], device(dims, y, x, z, 1 - c))]

    own = [
        pltpu.make_async_copy(shards[i], wholes[i].at[y, x, z, c], own_sem.at[i]) for i in range(n)
    ]
    for copy in own:
        copy.start()
    for copy in own:
        copy.wait()
    total = sum(counts)

    def start(copy):
        copy.start()

    def wait(copy):
        copy.wait()

    def either(g, one, other, act):
        late = lax.rem(g, 3) == 2
        for i in range(n):
            inside = jnp.logical_and(g >= bases[i], g < bases[i] + counts[i])

            @pl.when(jnp.logical_and(inside, jnp.logical_not(late)))
            def _():
                for copy in one(i, g - bases[i]):
                    act(copy)

            @pl.when(jnp.logical_and(inside, late))
            def _():
                for copy in other(i, g - bases[i]):
                    act(copy)

    def every(g, one, act):
        for i in range(n):

            @pl.when(jnp.logical_and(g >= bases[i], g < bases[i] + counts[i]))
            def _():
                for copy in one(i, g - bases[i]):
                    act(copy)

    def step(g, _):
        either(g, line_copies, own_copies, start)
        either(g - LAG, line_copies, own_copies, wait)
        either(g - LAG, first_copies, middle_copies, start)
        either(g - 2 * LAG, first_copies, middle_copies, wait)
        every(g - 2 * LAG, second_copies, start)
        every(g - 3 * LAG, second_copies, wait)
        every(g - 3 * LAG, core_copies, start)
        every(g - 4 * LAG, core_copies, wait)
        return 0

    lax.fori_loop(0, total + 4 * LAG, step, 0)


def gather_call(dims, shards, wides, collective_id):
    Y, X, Z = dims
    n = len(shards)
    dma = lambda *shape: pltpu.SemaphoreType.DMA(shape)
    most = max(X + Y - 2, 2 * (Z - 1), 1)
    wholes = pl.pallas_call(
        functools.partial(gather_kernel, dims, wides),
        out_shape=[
            jax.ShapeDtypeStruct((Y, X, Z, 2) + shard.shape, shard.dtype) for shard in shards
        ],
        in_specs=[pl.BlockSpec(memory_space=pltpu.VMEM)] * n,
        out_specs=[pl.BlockSpec(memory_space=pl.ANY)] * n,
        scratch_shapes=[
            dma(n),
            dma(AHEAD, most), dma(AHEAD, most),
            dma(AHEAD, most), dma(AHEAD, most),
            dma(AHEAD, most), dma(AHEAD, most),
            dma(AHEAD), dma(AHEAD),
        ],
        compiler_params=pltpu.CompilerParams(
            collective_id=collective_id, has_side_effects=True
        ),
    )(*shards)
    return [whole.reshape(-1, whole.shape[-1]) for whole in wholes]


def gather_all(shard):
    return lax.all_gather(shard, ALL, axis=0, tiled=True)


def scatter_all(whole):
    return lax.psum_scatter(whole, ALL, scatter_dimension=0, tiled=True)


def shards(
    inputs,
    segment_ids,
    cotangent,
    mixer_gain,
    input_proj,
    forget_proj,
    gate_proj,
    floor_log,
    output_gain,
    output_proj,
    dense_gain,
    up_first,
    up_second,
    down_proj,
):
    width = inputs.shape[-1]
    hidden = up_first.shape[1]
    groups = inputs.shape[0] * inputs.shape[1]
    span_len = inputs.shape[2]
    rows_all = groups * span_len
    parts, place = lax.axis_size("seq"), lax.axis_index("seq")

    vectors = jnp.stack([mixer_gain, floor_log, output_gain, dense_gain], axis=1)
    vectors = jnp.pad(vectors, ((0, 0), (0, EXTRA - 4)))
    depth, deep = output_proj.shape[0], down_proj.shape[0]
    wide, narrow = 512, 256
    own_kernel = (
        depth % 16 == 0
        and deep % 16 == 0
        and parts % 2 == 0
        and width % wide == 0
        and hidden % wide == 0
    )
    dims = split_mesh(lax.axis_size("dp"), parts)
    mix_shard = jnp.concatenate([input_proj, forget_proj, gate_proj, vectors], axis=1)
    up_shard = jnp.concatenate([up_first, up_second], axis=1)
    if own_kernel:
        mix_full, out_full, up_full = gather_call(
            dims, [mix_shard, output_proj, up_shard], [256] * 3, 0
        )
    else:
        mix_full, out_full, up_full = [gather_all(a) for a in (mix_shard, output_proj, up_shard)]
    gains = mix_full[:, 3 * width : 3 * width + 4].T
    if own_kernel:
        down_proj, gains = lax.optimization_barrier((down_proj, gains))
    down_full = gather_all(down_proj)
    mixer_gain_all = gains[0:1].astype(jnp.float32)
    floor_all = gains[1:2].astype(jnp.float32)
    out_gain_all = gains[2:3].astype(jnp.float32)
    dense_gain_all = gains[3:4].astype(jnp.float32)

    seg = segment_ids.reshape(groups, span_len)
    before = lax.ppermute(seg[:, -1:], "seq", [(i, i + 1) for i in range(parts - 1)])
    before = jnp.where(place == 0, -1, before)
    link = (seg == jnp.concatenate([before, seg[:, :-1]], axis=1)).astype(jnp.float32)
    link = jnp.broadcast_to(link.reshape(rows_all, 1), (rows_all, LANES))

    flat = inputs.reshape(rows_all, width)
    scale_one = lax.rsqrt(jnp.mean(flat * flat, axis=1, keepdims=True) + norm_eps)
    scaled_one = flat * scale_one
    normed_one = (scaled_one * mixer_gain_all).astype(jnp.bfloat16)
    pre_all = dot(normed_one, mix_full)
    pre_input = pre_all[:, :width]
    pre_forget = pre_all[:, width : 2 * width]
    pre_gate = pre_all[:, 2 * width : 3 * width]

    products, partial_state = forward_scan(pre_all, floor_all, link, span_len, width)
    products = products.reshape(groups, span_len, width)
    ends = exchange(
        jnp.concatenate(
            [products[:, -1], partial_state.reshape(groups, span_len, width)[:, -1]], axis=0
        )
    )
    span_mults = ends[:, :groups]
    entering = entering_forward(span_mults, ends[:, groups:])
    states = products * entering[:, None, :] + partial_state.reshape(groups, span_len, width)
    states_flat = states.reshape(rows_all, width)
    state_scale = lax.rsqrt(jnp.mean(states_flat * states_flat, axis=1, keepdims=True) + norm_eps)
    normed_state = states_flat * state_scale
    gate_out = jax.nn.silu(pre_gate)
    mixed = (normed_state * out_gain_all * gate_out).astype(jnp.bfloat16)
    middle = flat + dot(mixed, out_full)
    scale_two = lax.rsqrt(jnp.mean(middle * middle, axis=1, keepdims=True) + norm_eps)
    scaled_two = middle * scale_two
    normed_two = (scaled_two * dense_gain_all).astype(jnp.bfloat16)
    up_both = dot(normed_two, up_full)
    up_one, up_two = up_both[:, :hidden], up_both[:, hidden:]
    activated = (jax.nn.silu(up_one) * up_two).astype(jnp.bfloat16)
    grad_flat = cotangent.reshape(rows_all, width)
    grad_dense = grad_flat.astype(jnp.bfloat16)
    down_part = contract_rows(activated, grad_dense).astype(jnp.bfloat16)
    down_full, down_part = lax.optimization_barrier((down_full, down_part))
    grad_act = contract_last(grad_dense, down_full)
    grad_up_one = (grad_act * up_two * silu_slope(up_one)).astype(jnp.bfloat16)
    grad_up_two = (grad_act * jax.nn.silu(up_one)).astype(jnp.bfloat16)
    grad_up = jnp.concatenate([grad_up_one, grad_up_two], axis=1)
    grad_normed_two = contract_last(grad_up, up_full)
    gain_two = jnp.sum(grad_normed_two * scaled_two, axis=0)
    grad_middle = grad_flat + norm_back(grad_normed_two * dense_gain_all, scaled_two, scale_two)
    grad_mixer = grad_middle.astype(jnp.bfloat16)
    grad_mix_in = contract_last(grad_mixer, out_full)
    gain_out = jnp.sum(grad_mix_in * normed_state * gate_out, axis=0)
    grad_pre_gate = (
        grad_mix_in * normed_state * out_gain_all * silu_slope(pre_gate)
    ).astype(jnp.bfloat16)
    grad_states = norm_back(grad_mix_in * out_gain_all * gate_out, normed_state, state_scale)

    local_grad, carry_mult, head_grad = backward_scan(
        grad_states, pre_all, floor_all, link, span_len, width
    )
    arriving = entering_backward(span_mults, exchange(head_grad))
    adjoint = (
        local_grad.reshape(groups, span_len, width)
        + carry_mult.reshape(groups, span_len, width) * arriving[:, None, :]
    ).reshape(rows_all, width)
    previous = jnp.concatenate([entering[:, None, :], states[:, :-1]], axis=1)
    previous = previous.reshape(rows_all, width) * link[:, :1]
    leak = jnp.exp(floor_all) * jax.nn.sigmoid(-pre_forget)
    grad_forget = adjoint * (previous - jax.nn.silu(pre_input))
    grad_pre_input = (adjoint * leak * silu_slope(pre_input)).astype(jnp.bfloat16)
    grad_pre_forget = (grad_forget * leak * jax.nn.sigmoid(pre_forget)).astype(jnp.bfloat16)
    floor_sum = -jnp.sum(grad_forget * leak, axis=0)
    grad_pre = jnp.concatenate(
        [
            grad_pre_input,
            grad_pre_forget,
            grad_pre_gate,
            jnp.zeros((rows_all, EXTRA), jnp.bfloat16),
        ],
        axis=1,
    )
    block_all = contract_last(grad_pre, mix_full)
    gain_one = jnp.sum(block_all * scaled_one, axis=0)
    input_grad = (
        grad_middle + norm_back(block_all * mixer_gain_all, scaled_one, scale_one)
    ).reshape(inputs.shape)

    low = jnp.bfloat16
    vector_sums = jnp.stack([gain_one, floor_sum, gain_out, gain_two], axis=1)
    vector_sums = jnp.pad(vector_sums, ((0, 0), (0, LANES - 4))).astype(low)
    if own_kernel:
        *grads, vector_terms, block_out = scatter_call(
            dims,
            depth,
            wide,
            [normed_one.T, mixed.T, normed_two.T],
            [0, 0, 0, 1, 2, 2],
            [grad_pre_input, grad_pre_forget, grad_pre_gate, grad_mixer, grad_up_one, grad_up_two],
            [width] * 4 + [hidden] * 2,
            vector_sums,
            (activated, down_full, middle),
            1,
        )
    else:
        block_out = middle + dot(activated, down_full)
        terms = scatter_all(
            jnp.concatenate(
                [
                    contract_rows(normed_one, grad_pre[:, : 3 * width]).astype(low),
                    contract_rows(mixed, grad_mixer).astype(low),
                    contract_rows(normed_two, grad_up).astype(low),
                    vector_sums,
                ],
                axis=1,
            )
        ).astype(jnp.float32)
        marks = [width, 2 * width, 3 * width, 4 * width]
        marks += [4 * width + hidden, 4 * width + 2 * hidden]
        *grads, vector_terms = jnp.split(terms, marks, axis=1)
    down_grad = scatter_all(down_part).astype(jnp.float32)
    return (
        block_out.reshape(inputs.shape),
        input_grad,
        vector_terms[:, 0],
        grads[0],
        grads[1],
        grads[2],
        vector_terms[:, 1],
        vector_terms[:, 2],
        grads[3],
        vector_terms[:, 3],
        grads[4],
        grads[5],
        down_grad,
    )


def solution(mesh):
    whole = P(None, "dp", "seq", None)
    vector = P(ALL)
    matrix = P(ALL, None)
    return jax.shard_map(
        shards,
        mesh=mesh,
        in_specs=(
            whole,
            P(None, "dp", "seq"),
            whole,
            vector,
            matrix,
            matrix,
            matrix,
            vector,
            vector,
            matrix,
            vector,
            matrix,
            matrix,
            matrix,
        ),
        out_specs=(
            whole,
            whole,
            vector,
            matrix,
            matrix,
            matrix,
            vector,
            vector,
            matrix,
            vector,
            matrix,
            matrix,
            matrix,
        ),
        check_vma=False,
    )
```
